32 devices in a mesh: groups: 1, orient: 8 (over z, core), cls: 4 (over y, x).
Axes of the slice: x: 2, y: 2, z: 4, core: 2. Of those that a mesh axis runs over, the one named last changes fastest.
Arguments:
- particles: bfloat16 [384, 33024], P(('groups', 'orient', 'cls')), may hold values from -300 to 300
- projections: bfloat16 [8, 8, 33024], P('cls', 'orient')
- ctf: bfloat16 [8, 16512], replicated, may hold values from -1 to 1
- defocus_group: int32 [384], P(('groups', 'orient', 'cls')), may hold values from 0 to 7
- offsets: int32 [384, 2], P(('groups', 'orient', 'cls')), may hold values from -8 to 8
- routes: int32 [384, 4], P(('groups', 'orient', 'cls')), may hold values from 0 to 7, all different within a row; in each aligned block of 12 rows (0 to 11, 12 to 23, ...) at most 6 rows name the same one
Outputs:
- log_evidence: float32 [384], P(('groups', 'orient', 'cls'))
- data_sum: bfloat16 [8, 8, 33024], P(('groups', 'cls'), 'orient')
The draws below stay inside these ranges and needn't reach their ends.
Inputs may be any that keep to these rules, and one draw needn't show every extreme that they name: `routes`: the 4 blocks of a particle differ; among the particles of one device no block is listed more than 6 times, and some block is listed exactly 6 times.
All inputs are finite; a program needn't handle non-finite values.
Results may differ from the reference program's by a relative error of at most 0.01.
The reference program's roundings to bfloat16 on the way count: a program that leaves them out, or rounds other values in their place, can miss the bound.
Values may be sent and summed in bfloat16 or wider, within the bound.
No kernel may reach another device: no remote copies, remote signals or barrier semaphores. Data moves between devices by JAX's collectives and lax.ppermute only.
A program may use at most 64 MiB of HBM per device.

```python
import math
import jax
import jax.numpy as jnp
import numpy as np
from jax import lax

KX = 86
KY = 192
BOX = 256
PIX = 16512
NDEF = 8
TOPK = 4
CLASSES = 8
ORI_DEV = 1
DIRECTIONS = 8
PART_DEV = 12
PARTICLES = 384
CAP = 6
N_ORIENT = 8
N_CLS = 4


def draw_particles(key, part):
    first_key = jax.random.fold_in(key, 0)
    shape = (PARTICLES, 2 * PIX)
    values = jnp.clip(jax.random.normal(first_key, shape, jnp.float32), -6.0, 6.0)
    return values.astype(jnp.bfloat16)


def draw_projections(key, part):
    first_key, second_key = jax.random.split(key)
    shape = (CLASSES, DIRECTIONS, 2 * PIX)
    values = jnp.clip(jax.random.normal(first_key, shape, jnp.float32), -6.0, 6.0)
    amplitude = jnp.exp(jax.random.uniform(second_key, (CLASSES, DIRECTIONS, 1), jnp.float32, 0.0, math.log(3.0)))
    return (values * amplitude * (1.0 / math.sqrt(2.0 * PIX))).astype(jnp.bfloat16)


def set_ends(drawn, rng, low, high):
    place = [jax.random.randint(jax.random.fold_in(rng, axis), (), 0, length) for axis, length in enumerate(drawn.shape)]
    widest = drawn.shape.index(max(drawn.shape))
    next_to = place[:widest] + [(place[widest] + 1) % drawn.shape[widest]] + place[widest + 1:]
    return drawn.at[tuple(place)].set(low).at[tuple(next_to)].set(high)


def deal_out(stream_key, own, number, rows, number_of, top, bound, slope):
    ranking = jax.random.permutation(stream_key, number_of)
    crowded, usual = portions_of(number_of, rows * top, bound, slope, True), portions_of(number_of, rows * top, bound, slope, False)
    places = jnp.arange(number_of)

    def named(lengths, offset_by):
        used = int((lengths > 0).sum())
        fixed = max(1, used // 4)
        passed = fixed + (places - fixed + offset_by * (used - fixed)) % max(1, number_of - fixed)
        return jnp.zeros((number_of,), jnp.int32).at[ranking[jnp.where(places < fixed, places, passed)]].set(jnp.asarray(lengths, jnp.int32))

    lengths = jnp.where(number % 4 == 0, named(crowded, number // 4), named(usual, number - number // 4 - 1))
    mixed = jax.random.permutation(jax.random.fold_in(own, 3), number_of)
    source_of, sink = mixed[0:number_of // 2 * 2:2], mixed[1:number_of // 2 * 2:2]
    margin = jnp.minimum(lengths[source_of] - 1, bound - lengths[sink]) // 2
    margin = jnp.where((source_of == ranking[0]) | (sink == ranking[0]) | (lengths[sink] == 0), 0, jnp.maximum(margin, 0))
    passed = jax.random.randint(jax.random.fold_in(own, 4), (number_of // 2,), 0, 1 << 20) % (margin + 1)
    lengths = lengths.at[source_of].add(-passed).at[sink].add(passed)
    labels = jnp.searchsorted(jnp.cumsum(lengths), jnp.arange(rows * top), side="right").astype(jnp.int32)
    table = labels.reshape(top, rows).T
    table = table[jax.random.permutation(jax.random.fold_in(own, 1), rows)]
    offset_by = jax.random.randint(jax.random.fold_in(own, 2), (rows, 1), 0, top)
    return jnp.take_along_axis(table, (jnp.arange(top)[None, :] + offset_by) % top, axis=1)


def portions_of(number_of, total, bound, lean, full):
    portions = [(1 << 20) // math.isqrt(grade ** lean) + 1 for grade in range(1, number_of + 1)]
    largest = bound if full else min(bound, max(-(-total // number_of), total * portions[0] // sum(portions)))
    least = 1 if total - largest >= number_of - 1 else 0
    given, rest = [largest] + [least] * (number_of - 1), total - largest - least * (number_of - 1)
    while rest > 0:
        candidates = [i for i in range(1, number_of) if given[i] < largest] or [i for i in range(1, number_of) if given[i] < bound]
        pool, remaining = sum([portions[i] for i in candidates]), rest
        for i in candidates:
            more = min(bound - given[i], max(1, remaining * portions[i] // pool), rest)
            given[i] = given[i] + more
            rest = rest - more
    return np.array(given)


def setup_inputs(seed: int = 0, part: int = 0) -> dict:
    key_of = jax.random.split(jax.random.key(seed), 7)
    part_splits = jax.random.split(jax.random.fold_in(key_of[6], part), 7)
    particles = draw_particles(jax.random.fold_in(jax.random.fold_in(key_of[6], part), 71), part)
    projections = draw_projections(jax.random.fold_in(key_of[6], 71), part)
    ctf = jnp.clip(jax.random.uniform(key_of[2], (NDEF, PIX), jnp.float32, -1.0, 1.0), -1.0, 1.0).astype(jnp.bfloat16)
    defocus_group = set_ends(jax.random.randint(part_splits[3], (PARTICLES,), 0, NDEF), jax.random.fold_in(part_splits[3], 1), 0, NDEF - 1).astype(jnp.int32)
    offsets = set_ends(jax.random.randint(part_splits[4], (PARTICLES, 2), -8, 9), jax.random.fold_in(part_splits[4], 1), -8, 8).astype(jnp.int32)
    routes_keys = jax.random.split(jax.random.fold_in(part_splits[5], 1), PARTICLES // PART_DEV)
    routes_turns = jax.random.permutation(jax.random.fold_in(part_splits[5], 3), PARTICLES // PART_DEV)
    routes = jax.vmap(lambda own, number: deal_out(jax.random.fold_in(part_splits[5], 2), own, number, PART_DEV, N_ORIENT, TOPK, CAP, 2))(routes_keys, routes_turns).reshape((PARTICLES, TOPK))
    return dict(particles=particles, projections=projections, ctf=ctf, defocus_group=defocus_group, offsets=offsets, routes=routes)


two_pi = 2.0 * math.pi
highest = lax.Precision.HIGHEST
local_across = np.array([0, 1, -1, 0, 0], dtype=np.int32)
local_down = np.array([0, 0, 0, 1, -1], dtype=np.int32)


def frequencies():
    column = jnp.arange(KX * KY, dtype=jnp.int32)
    return column // KY, column % KY - KY // 2


def rotation(shift_across, shift_down, freq_across, freq_down):
    turns = jnp.mod(freq_across * shift_across + freq_down * shift_down, BOX)
    angle = turns.astype(jnp.float32) * (two_pi / BOX)
    return jnp.cos(angle), jnp.sin(angle)


def combine_stats(peaks, masses):
    top_value = jnp.max(peaks, axis=-1, keepdims=True)
    return top_value[..., 0] + jnp.log(jnp.sum(masses * jnp.exp(peaks - top_value), axis=-1))


def align_images(images, ctf_rows, shifts, freq_across, freq_down, pixel_count):
    real_part = images[:, :pixel_count].astype(jnp.float32)
    imag_part = images[:, pixel_count:].astype(jnp.float32)
    cos_base, sin_base = rotation(shifts[:, 0:1], shifts[:, 1:2], freq_across[None, :], freq_down[None, :])
    first = (real_part * cos_base + imag_part * sin_base) * ctf_rows
    second = (imag_part * cos_base - real_part * sin_base) * ctf_rows
    return jnp.concatenate([first, second], axis=1).astype(jnp.bfloat16)


def spread_phase(table, ndim_rest):
    return table.reshape((table.shape[0],) + (1,) * ndim_rest + (table.shape[1],))


def turn_refs(ref_block, cos_shift, sin_shift, pixel_count):
    real_ref = ref_block[..., :pixel_count].astype(jnp.float32)
    imag_ref = ref_block[..., pixel_count:].astype(jnp.float32)
    cos_wide = spread_phase(cos_shift, real_ref.ndim - 1)
    sin_wide = spread_phase(sin_shift, real_ref.ndim - 1)
    first = real_ref[None] * cos_wide - imag_ref[None] * sin_wide
    second = real_ref[None] * sin_wide + imag_ref[None] * cos_wide
    turned = jnp.concatenate([first, second], axis=-1).astype(jnp.bfloat16)
    return turned, real_ref * real_ref + imag_ref * imag_ref


def back_rotate(summed, cos_shift, sin_shift, pixel_count):
    cos_wide = spread_phase(cos_shift, summed.ndim - 2)
    sin_wide = spread_phase(sin_shift, summed.ndim - 2)
    real_sum = summed[..., :pixel_count]
    imag_sum = summed[..., pixel_count:]
    first = jnp.sum(real_sum * cos_wide + imag_sum * sin_wide, axis=0)
    second = jnp.sum(imag_sum * cos_wide - real_sum * sin_wide, axis=0)
    return jnp.concatenate([first, second], axis=-1)


def reference(particles, projections, ctf, defocus_group, offsets, routes):
    pixel_count = KX * KY
    freq_across, freq_down = frequencies()
    ctf_table = ctf.astype(jnp.float32)
    group_total = PARTICLES // PART_DEV

    def base_group(inputs):
        images, group_ids, shifts = inputs
        return align_images(images, ctf_table[group_ids], shifts, freq_across, freq_down, pixel_count)

    aligned = lax.map(base_group, (particles.reshape(group_total, PART_DEV, 2 * pixel_count),
                                   defocus_group.reshape(group_total, PART_DEV),
                                   offsets.reshape(group_total, PART_DEV, 2)))
    aligned = aligned.reshape(PARTICLES, 2 * pixel_count)
    cos_shift, sin_shift = rotation(jnp.asarray(local_across, dtype=jnp.int32)[:, None],
                                    jnp.asarray(local_down, dtype=jnp.int32)[:, None],
                                    freq_across[None, :], freq_down[None, :])
    real_all = projections[..., :pixel_count].astype(jnp.float32)
    imag_all = projections[..., pixel_count:].astype(jnp.float32)
    magnitude = real_all * real_all + imag_all * imag_all
    energy = jnp.einsum('gj,cdj->gcd', ctf_table * ctf_table, magnitude, precision=highest)
    row_of = (jnp.arange(PARTICLES, dtype=jnp.int32) // PART_DEV) % N_CLS
    flat_routes = routes.reshape(-1)
    flat_rows = jnp.repeat(row_of, TOPK)
    entry_total = PARTICLES * TOPK
    limit = CAP * N_ORIENT
    shift_total = cos_shift.shape[0]

    def block_scores(block_index):
        ref_block = lax.dynamic_slice_in_dim(projections, block_index * ORI_DEV, ORI_DEV, 1)
        turned, unused_mag = turn_refs(ref_block, cos_shift, sin_shift, pixel_count)
        turned_flat = turned.reshape(-1, 2 * pixel_count)
        block_energy = lax.dynamic_slice_in_dim(energy, block_index * ORI_DEV, ORI_DEV, 2)
        orders_all, occupied_all, scores_all = [], [], []
        for cls_row in range(N_CLS):
            matches = (flat_routes == block_index) & (flat_rows == cls_row)
            chosen_order = jnp.argsort(jnp.where(matches, 0, 1).astype(jnp.int32), stable=True)[:limit].astype(jnp.int32)
            occupied = matches[chosen_order].astype(jnp.float32)
            owners = chosen_order // TOPK
            rows_used = aligned[owners]
            products = lax.dot_general(rows_used, turned_flat, (((1,), (1,)), ((), ())), preferred_element_type=jnp.float32)
            slot_energy = block_energy[defocus_group[owners]]
            score = products.reshape(limit, shift_total, CLASSES, ORI_DEV) - 0.5 * slot_energy[:, None]
            orders_all.append(chosen_order)
            occupied_all.append(occupied)
            scores_all.append(score)
        return jnp.stack(orders_all), jnp.stack(occupied_all), jnp.stack(scores_all)

    orders, occupieds, scores = lax.map(block_scores, jnp.arange(N_ORIENT, dtype=jnp.int32))
    peaks = jnp.max(scores, axis=(3, 4, 5))
    masses = jnp.sum(jnp.exp(scores - peaks[..., None, None, None]), axis=(3, 4, 5))
    target = jnp.where(occupieds > 0, orders, entry_total).reshape(-1)
    entry_peak = jnp.zeros((entry_total,), jnp.float32).at[target].set(peaks.reshape(-1), mode="drop")
    entry_mass = jnp.zeros((entry_total,), jnp.float32).at[target].set(masses.reshape(-1), mode="drop")
    log_evidence = combine_stats(entry_peak.reshape(PARTICLES, TOPK), entry_mass.reshape(PARTICLES, TOPK))

    def block_sums(inputs):
        block_orders, block_occupied, block_scores_in = inputs
        running = jnp.zeros((CLASSES, ORI_DEV, 2 * pixel_count), jnp.float32)
        for cls_row in range(N_CLS):
            owners = block_orders[cls_row] // TOPK
            rows_used = aligned[owners]
            evidence = log_evidence[owners]
            live = (block_occupied[cls_row] > 0)[:, None, None, None]
            exponent = jnp.where(live, block_scores_in[cls_row] - evidence[:, None, None, None], 0.0)
            weights = jnp.where(live, jnp.exp(exponent), 0.0).astype(jnp.bfloat16)
            summed = lax.dot_general(weights.reshape(limit, -1), rows_used, (((0,), (0,)), ((), ())),
                                     preferred_element_type=jnp.float32)
            summed = summed.reshape(shift_total, CLASSES, ORI_DEV, 2 * pixel_count)
            partial_value = back_rotate(summed, cos_shift, sin_shift, pixel_count).astype(jnp.bfloat16)
            partial_value = lax.optimization_barrier(partial_value)
            running = running + partial_value.astype(jnp.float32)
        return running.astype(jnp.bfloat16)

    sums = lax.map(block_sums, (orders, occupieds, scores))
    data_sum = jnp.transpose(sums, (1, 0, 2, 3)).reshape(CLASSES, DIRECTIONS, 2 * pixel_count)
    return (log_evidence, data_sum)
```

```python
import functools
import math

import jax
import jax.numpy as jnp
from jax import lax
from jax.experimental import pallas as pl
from jax.experimental.pallas import tpu as pltpu
from jax.sharding import Mesh
from jax.sharding import PartitionSpec as P

KX = 86
KY = 192
BOX = 256
LANES = 128
SHIFTS = 5

highest = lax.Precision.HIGHEST
f32 = jnp.float32
bf16 = jnp.bfloat16


def unit_circle(turns):
    quarter = BOX // 4
    quadrant = jnp.floor(turns * (1.0 / quarter) + 0.5)
    angle = (turns - quadrant * quarter) * (2.0 * math.pi / BOX)
    quadrant = quadrant - 4.0 * jnp.floor(quadrant * 0.25)
    square = angle * angle
    sine = angle * (
        1.0
        + square
        * (-1.0 / 6 + square * (1.0 / 120 + square * (-1.0 / 5040 + square * (1.0 / 362880))))
    )
    cosine = 1.0 + square * (
        -0.5 + square * (1.0 / 24 + square * (-1.0 / 720 + square * (1.0 / 40320)))
    )
    odd = (quadrant == 1.0) | (quadrant == 3.0)
    first = jnp.where(odd, sine, cosine)
    second = jnp.where(odd, cosine, sine)
    first = jnp.where((quadrant == 1.0) | (quadrant == 2.0), -first, first)
    second = jnp.where(quadrant >= 2.0, -second, second)
    return first, second


def align_kernel(
    pixel_count, width, images, ctf, group, offsets, routes, out, ctf_rows
):
    rows = images.shape[0]
    pieces = out.shape[0]
    route_count = routes.shape[1]
    block = math.lcm(LANES, KY)
    per_block = block // LANES
    onehot = (
        group[...] == lax.broadcasted_iota(jnp.int32, (rows, ctf.shape[0]), 1)
    ).astype(bf16)
    ctf_rows[...] = jnp.dot(onehot, ctf[...], preferred_element_type=f32)
    shift_across = offsets[:, 0:1].astype(f32)
    shift_down = offsets[:, 1:2].astype(f32)
    lane = lax.broadcasted_iota(jnp.int32, (rows, block), 1)
    across = jnp.zeros((rows, block), jnp.int32)
    for step in range(1, block // KY):
        across = across + (lane >= step * KY).astype(jnp.int32)
    down = lane - across * KY - KY // 2
    base_cos, base_sin = unit_circle(
        across.astype(f32) * shift_across + down.astype(f32) * shift_down
    )
    blocks = -(-pixel_count // block)
    start = lax.broadcasted_iota(jnp.int32, (rows, blocks), 1) * (block // KY)
    start_cos, start_sin = unit_circle(start.astype(f32) * shift_across)
    for piece in range(pieces):
        for part in range(width // LANES):
            low = piece * width + part * LANES
            here = slice(part * LANES, (part + 1) * LANES)
            if low >= pixel_count:
                out[piece, :, here] = jnp.zeros((2 * rows, LANES), bf16)
                continue
            turn, step = divmod(low // LANES, per_block)
            bc = base_cos[:, step * LANES : (step + 1) * LANES]
            bs = base_sin[:, step * LANES : (step + 1) * LANES]
            rc = start_cos[:, turn : turn + 1]
            rs = start_sin[:, turn : turn + 1]
            cosine = bc * rc - bs * rs
            sine = bs * rc + bc * rs
            scale = ctf_rows[:, low : low + LANES]
            real = images[:, low : low + LANES].astype(f32)
            imag = images[:, pixel_count + low : pixel_count + low + LANES].astype(f32)
            first = (real * cosine + imag * sine) * scale
            second = (imag * cosine - real * sine) * scale
            out[piece, :, here] = jnp.concatenate([first, second], axis=0).astype(bf16)
    lane = lax.broadcasted_iota(jnp.int32, (rows, LANES), 1)
    notes = jnp.where(lane == route_count, group[...], 0)
    for r in range(route_count):
        notes = jnp.where(lane == r, routes[:, r : r + 1], notes)
    notes = notes.astype(f32)
    notes = jnp.concatenate([notes, notes], axis=0).astype(bf16)
    for piece in range(pieces):
        out[piece, :, width : width + LANES] = notes


def score_kernel(rows, route_count, aligned, refs, ctf, phases, out, turned, power):
    width = phases.shape[1]
    owners = refs.shape[0]
    held = refs.shape[1] // (2 * width)
    total = held * owners
    for low in range(0, width, LANES):
        here = slice(low, low + LANES)

        def take(half):
            return jnp.concatenate(
                [
                    refs[:, (2 * k + half) * width + low : (2 * k + half) * width + low + LANES]
                    for k in range(held)
                ],
                axis=0,
            )

        real, imag = take(0), take(1)
        turned[0, 0:total, here] = real
        turned[1, 0:total, here] = imag
        real, imag = real.astype(f32), imag.astype(f32)
        power[:, here] = real * real + imag * imag
        for axis in range(2):
            cosine = phases[2 * axis : 2 * axis + 1, here]
            sine = phases[2 * axis + 1 : 2 * axis + 2, here]
            rc, rs, ic, is_ = real * cosine, real * sine, imag * cosine, imag * sine
            at = (1 + 2 * axis) * total
            turned[0, at : at + total, here] = (rc - is_).astype(bf16)
            turned[1, at : at + total, here] = (rs + ic).astype(bf16)
            at = at + total
            turned[0, at : at + total, here] = (rc + is_).astype(bf16)
            turned[1, at : at + total, here] = (ic - rs).astype(bf16)
    across = (((1,), (1,)), ((), ()))
    images = aligned[:, 0:width]
    real = lax.dot_general(images, turned[0], across, preferred_element_type=f32)
    imag = lax.dot_general(images, turned[1], across, preferred_element_type=f32)
    table = ctf[...].astype(f32)
    energy = lax.dot_general(
        table * table, power[...], across, precision=highest, preferred_element_type=f32
    )
    energy = jnp.concatenate([energy] * SHIFTS, axis=1) * 0.5
    group = aligned[:, width : width + LANES].astype(f32)[:, route_count : route_count + 1]
    for g in range(table.shape[0]):
        real = real - jnp.where(group == float(g), energy[g : g + 1, :], 0.0)
    for source in range(aligned.shape[0] // (2 * rows)):
        at = 2 * rows * source
        out[source * rows : (source + 1) * rows, :] = (
            real[at : at + rows, :] + imag[at + rows : at + 2 * rows, :]
        )


def sums_kernel(rows, route_count, per_direction, scores, aligned, phases, out, evidence, wide):
    width = phases.shape[1]
    count = aligned.shape[0]
    owners = out.shape[0]
    held = out.shape[1] // (2 * width)
    total = held * owners
    for source in range(count // (2 * rows)):
        values = scores[source * rows : (source + 1) * rows, :]
        at = 2 * rows * source
        wide[at : at + rows, :] = values
        wide[at + rows : at + 2 * rows, :] = values
    values = wide[...]
    notes = aligned[:, width : width + LANES].astype(f32)
    lane = lax.broadcasted_iota(jnp.int32, (1, SHIFTS * total), 1)
    direction = (lax.rem(lane, owners) // per_direction).astype(f32)
    listed = notes[:, 0:1] == direction
    for r in range(1, route_count):
        listed = listed | (notes[:, r : r + 1] == direction)
    masked = jnp.where(listed, values, -jnp.inf)
    peak = jnp.max(masked, axis=1, keepdims=True)
    mass = jnp.sum(jnp.where(listed, jnp.exp(values - peak), 0.0), axis=1, keepdims=True)
    log_evidence = peak + jnp.log(mass)
    evidence[...] = jnp.broadcast_to(log_evidence, evidence.shape)
    exponent = jnp.where(listed, values - log_evidence, 0.0)
    weights = jnp.where(listed, jnp.exp(exponent), 0.0)
    row = lax.broadcasted_iota(jnp.int32, (count, 1), 0)
    first_half = jnp.zeros((count, 1), jnp.bool_)
    for source in range(count // (2 * rows)):
        at = 2 * rows * source
        first_half = first_half | ((row >= at) & (row < at + rows))
    weights_real = jnp.where(first_half, weights, 0.0).T.astype(bf16)
    weights_imag = jnp.where(first_half, 0.0, weights).T.astype(bf16)
    step = 2 * LANES
    for low in range(0, width, step):
        high = min(low + step, width)
        images = aligned[:, low:high]
        real = jnp.dot(weights_real, images, preferred_element_type=f32)
        imag = jnp.dot(weights_imag, images, preferred_element_type=f32)
        u = [real[t * total : (t + 1) * total] for t in range(SHIFTS)]
        v = [imag[t * total : (t + 1) * total] for t in range(SHIFTS)]
        first, second = u[0], v[0]
        for axis in range(2):
            cosine = phases[2 * axis : 2 * axis + 1, low:high]
            sine = phases[2 * axis + 1 : 2 * axis + 2, low:high]
            one, two = 1 + 2 * axis, 2 + 2 * axis
            first = first + (u[one] + u[two]) * cosine + (v[one] - v[two]) * sine
            second = second + (v[one] + v[two]) * cosine - (u[one] - u[two]) * sine
        first, second = first.astype(bf16), second.astype(bf16)
        for k in range(held):
            mine = slice(k * owners, (k + 1) * owners)
            out[:, 2 * k * width + low : 2 * k * width + high] = first[mine]
            out[:, (2 * k + 1) * width + low : (2 * k + 1) * width + high] = second[mine]


def per_device(particles, projections, ctf, defocus_group, offsets, routes):
    pixel_count = KX * KY
    rows = particles.shape[0]
    route_count = routes.shape[1]
    held = projections.shape[0] * projections.shape[1]
    depth, cores, columns = (lax.axis_size(name) for name in ("depth", "core", "cls"))
    plane = ("core", "cls")
    everyone = ("depth", "core", "cls")
    pieces = cores * columns
    owners = depth * pieces
    width = -(-pixel_count // (pieces * LANES)) * LANES
    padded = pieces * width
    place = lax.axis_index(plane)

    refs = projections.reshape(2 * held, pixel_count)
    refs = jnp.pad(refs, ((0, 0), (0, padded - pixel_count)))
    refs = refs.reshape(2 * held, pieces, width).transpose(1, 0, 2).reshape(1, pieces, -1)
    refs = jnp.broadcast_to(refs, (depth, pieces, 2 * held * width)).reshape(owners, -1)
    refs = lax.all_to_all(refs, everyone, split_axis=0, concat_axis=0, tiled=True)

    aligned = pl.pallas_call(
        functools.partial(align_kernel, pixel_count, width),
        out_shape=jax.ShapeDtypeStruct((pieces, 2 * rows, width + LANES), bf16),
        scratch_shapes=[pltpu.VMEM((rows, pixel_count), f32)],
        cost_estimate=pl.CostEstimate(flops=4000000, bytes_accessed=2000000, transcendentals=0),
        name="align",
    )(particles, ctf, defocus_group[:, None], offsets, routes)
    aligned = lax.all_to_all(aligned, plane, split_axis=0, concat_axis=0, tiled=True)
    aligned = aligned.reshape(pieces * 2 * rows, width + LANES)

    column = place * width + jnp.arange(width, dtype=jnp.int32)
    across, down = column // KY, column % KY - KY // 2
    angles = jnp.stack([across, down]).astype(f32) * (2.0 * math.pi / BOX)
    phases = jnp.stack([jnp.cos(angles), jnp.sin(angles)], axis=1).reshape(4, width)
    ctf_here = lax.dynamic_slice_in_dim(
        jnp.pad(ctf, ((0, 0), (0, padded - pixel_count))), place * width, width, 1
    )

    total = held * owners
    scores = pl.pallas_call(
        functools.partial(score_kernel, rows, route_count),
        out_shape=jax.ShapeDtypeStruct((pieces * rows, SHIFTS * total), f32),
        scratch_shapes=[
            pltpu.VMEM((2, SHIFTS * total, width), bf16),
            pltpu.VMEM((total, width), f32),
        ],
        name="score",
    )(aligned, refs, ctf_here, phases)

    span = 1
    while span < cores:
        scores = scores + lax.ppermute(scores, "core", [(i, i ^ span) for i in range(cores)])
        span *= 2
    span = 1
    while span < columns:
        scores = scores + lax.ppermute(scores, "cls", [(i, i ^ span) for i in range(columns)])
        span *= 2

    sums, evidence = pl.pallas_call(
        functools.partial(sums_kernel, rows, route_count, pieces // cores),
        out_shape=(
            jax.ShapeDtypeStruct((owners, 2 * held * width), bf16),
            jax.ShapeDtypeStruct((2 * pieces * rows, LANES), f32),
        ),
        scratch_shapes=[pltpu.VMEM((2 * pieces * rows, SHIFTS * total), f32)],
        name="sums",
    )(scores, aligned, phases)
    log_evidence = lax.dynamic_slice_in_dim(evidence, place * 2 * rows, rows, 0)[:, 0]

    sums = lax.all_to_all(sums, everyone, split_axis=0, concat_axis=0, tiled=True)
    data_sum = jnp.sum(sums.reshape(depth, pieces, 2 * held * width).astype(f32), axis=0)
    data_sum = data_sum.astype(bf16).reshape(pieces, 2 * held, width).transpose(1, 0, 2)
    data_sum = data_sum.reshape(2 * held, padded)[:, :pixel_count]
    return (log_evidence, data_sum.reshape(projections.shape))


def solution(mesh):
    groups, orient, columns = (mesh.shape[name] for name in ("groups", "orient", "cls"))
    cores = 2 if orient % 2 == 0 else 1
    inner = Mesh(
        mesh.devices.reshape(groups, orient // cores, cores, columns),
        ("groups", "depth", "core", "cls"),
    )
    spread = ("groups", "depth", "core", "cls")
    placed = (
        P(spread, None),
        P("cls", ("depth", "core"), None),
        P(),
        P(spread),
        P(spread, None),
        P(spread, None),
    )
    return jax.shard_map(
        per_device,
        mesh=inner,
        in_specs=placed,
        out_specs=(P(spread), P(("groups", "cls"), ("depth", "core"), None)),
        check_vma=False,
    )
```

```python
import functools
import math

import jax
import jax.numpy as jnp
from jax import lax
from jax.experimental import pallas as pl
from jax.experimental.pallas import tpu as pltpu
from jax.sharding import Mesh
from jax.sharding import PartitionSpec as P


KX = 86
KY = 192
BOX = 256
LANES = 128
SHIFTS = 5

highest = lax.Precision.HIGHEST
f32 = jnp.float32
bf16 = jnp.bfloat16


def unit_circle(turns):
    quarter = BOX // 4
    quadrant = jnp.floor(turns * (1.0 / quarter) + 0.5)
    angle = (turns - quadrant * quarter) * (2.0 * math.pi / BOX)
    quadrant = quadrant - 4.0 * jnp.floor(quadrant * 0.25)
    square = angle * angle
    sine = angle * (
        1.0
        + square
        * (-1.0 / 6 + square * (1.0 / 120 + square * (-1.0 / 5040 + square * (1.0 / 362880))))
    )
    cosine = 1.0 + square * (
        -0.5 + square * (1.0 / 24 + square * (-1.0 / 720 + square * (1.0 / 40320)))
    )
    odd = (quadrant == 1.0) | (quadrant == 3.0)
    first = jnp.where(odd, sine, cosine)
    second = jnp.where(odd, cosine, sine)
    first = jnp.where((quadrant == 1.0) | (quadrant == 2.0), -first, first)
    second = jnp.where(quadrant >= 2.0, -second, second)
    return first, second


def other(place, step, size):
    if size & (size - 1) == 0:
        return place ^ step
    return lax.rem(place + step, size)


def source(place, step, size):
    if size & (size - 1) == 0:
        return place ^ step
    return lax.rem(place + size - step, size)


def exchange_order(step):
    return (step.bit_count() == 2, -step.bit_count(), step)


def routes_of(step, size):
    return [(i, int(other(i, step, size))) for i in range(size)]


def split_refs(pixel_count, width, refs, out):
    held = refs.shape[0]
    pieces = -(-pixel_count // width)
    for piece in range(pieces):
        low = piece * width
        size = min(width, pixel_count - low)
        for half in range(2):
            values = refs[:, half * pixel_count + low : half * pixel_count + low + size]
            for copy in range(piece, out.shape[0], pieces):
                out[copy, half * held : (half + 1) * held, 0:size] = values
                if size < width:
                    out[copy, half * held : (half + 1) * held, size:width] = jnp.zeros(
                        (held, width - size), bf16
                    )


def prepare_kernel(pixel_count, width, steps, *refs):
    distant, (place, split), rest = refs[:6], refs[6:8], refs[8:]
    outs, near, (ctf_rows, whole, table, arrived) = rest[: len(steps)], rest[len(steps) : -4], rest[-4:]
    copies = [
        pltpu.make_async_copy(far, here, arrived.at[i])
        for i, (far, here) in enumerate(zip(distant, near))
    ]
    for copy in copies:
        copy.start()
    copies[0].wait()
    split_refs(pixel_count, width, near[0], split)
    for copy in copies[1:]:
        copy.wait()
    align(pixel_count, width, steps, *near[1:], place, outs, ctf_rows, whole, table)


def align(
    pixel_count, width, steps, images, ctf, groups, offsets, routes, place, outs, ctf_rows, whole, table
):
    rows = images.shape[0]
    pieces = len(outs)
    route_count = routes.shape[0]
    table[...] = jnp.zeros(table.shape, f32)
    table[0:2, 0:rows] = offsets[...].astype(f32)
    table[2:3, 0:rows] = groups[...].astype(f32)
    table[3 : 3 + route_count, 0:rows] = routes[...].astype(f32)
    facts = table[...].T[0:rows]
    shift_across, shift_down, group = facts[:, 0:1], facts[:, 1:2], facts[:, 2:3]
    block = math.lcm(LANES, KY)
    per_block = block // LANES
    onehot = (
        group == lax.broadcasted_iota(jnp.int32, (rows, ctf.shape[0]), 1).astype(f32)
    ).astype(bf16)
    ctf_rows[...] = jnp.dot(onehot, ctf[...], preferred_element_type=f32)
    lane = lax.broadcasted_iota(jnp.int32, (rows, block), 1)
    across = jnp.zeros((rows, block), jnp.int32)
    for step in range(1, block // KY):
        across = across + (lane >= step * KY).astype(jnp.int32)
    down = lane - across * KY - KY // 2
    base_cos, base_sin = unit_circle(
        across.astype(f32) * shift_across + down.astype(f32) * shift_down
    )
    blocks = -(-pixel_count // block)
    start = lax.broadcasted_iota(jnp.int32, (rows, blocks), 1) * (block // KY)
    start_cos, start_sin = unit_circle(start.astype(f32) * shift_across)
    for piece in range(pieces):
        for part in range(width // LANES):
            low = piece * width + part * LANES
            here = slice(part * LANES, (part + 1) * LANES)
            if low >= pixel_count:
                whole[piece, :, here] = jnp.zeros((2 * rows, LANES), bf16)
                continue
            turn, step = divmod(low // LANES, per_block)
            bc = base_cos[:, step * LANES : (step + 1) * LANES]
            bs = base_sin[:, step * LANES : (step + 1) * LANES]
            rc = start_cos[:, turn : turn + 1]
            rs = start_sin[:, turn : turn + 1]
            cosine = bc * rc - bs * rs
            sine = bs * rc + bc * rs
            scale = ctf_rows[:, low : low + LANES]
            real = images[:, low : low + LANES].astype(f32)
            imag = images[:, pixel_count + low : pixel_count + low + LANES].astype(f32)
            first = (real * cosine + imag * sine) * scale
            second = (imag * cosine - real * sine) * scale
            whole[piece, :, here] = jnp.concatenate([first, second], axis=0).astype(bf16)
    lane = lax.broadcasted_iota(jnp.int32, (rows, LANES), 1)
    notes = jnp.where(lane == route_count, group, 0.0)
    for r in range(route_count):
        notes = jnp.where(lane == r, facts[:, 3 + r : 4 + r], notes)
    notes = jnp.concatenate([notes, notes], axis=0).astype(bf16)
    for step, out in zip(steps, outs):
        out[:, 0:width] = whole[other(place[0], step, pieces)]
        out[:, width : width + LANES] = notes


def lane_facts(total, owners, same_core, columns, core_here):
    lane = lax.broadcasted_iota(jnp.int32, (1, SHIFTS * total), 1)
    owner = lax.rem(lane, owners)
    core = source(core_here, owner // same_core, owners // same_core)
    direction = (lax.rem(owner, same_core) // columns) * (owners // same_core) + core
    shift, held = lane // total, lax.rem(lane, total) // owners
    spot = (shift * (total // owners) + held) * columns + lax.rem(owner, columns)
    return direction.astype(f32), spot.astype(f32)


def spot_table(spot, spots):
    row = lax.broadcasted_iota(jnp.int32, (spots, spot.shape[1]), 0).astype(f32)
    return jnp.where(row == spot, 1.0, 0.0).astype(bf16)


def score_kernel(rows, route_count, columns, steps, *refs_all):
    count = len(steps)
    parts = refs_all[:count]
    *blocks, ctf, phases, place, out, aligned, turned, power, dense, notes = refs_all[count:]
    same_core = blocks[0].shape[1]
    owners = len(blocks) * same_core
    width = phases.shape[1]
    held = blocks[0].shape[0] // 2
    total = held * len(blocks) * blocks[0].shape[1]
    for step, part in zip(steps, parts):
        aligned[source(place[0], step, count)] = part[...]
    for low in range(0, width, LANES):
        here = slice(low, low + LANES)
        real = jnp.concatenate(
            [block[k, :, here] for k in range(held) for block in blocks], axis=0
        )
        imag = jnp.concatenate(
            [block[held + k, :, here] for k in range(held) for block in blocks], axis=0
        )
        turned[0, 0:total, here] = real
        turned[1, 0:total, here] = imag
        real, imag = real.astype(f32), imag.astype(f32)
        power[:, here] = real * real + imag * imag
        for axis in range(2):
            cosine = phases[2 * axis : 2 * axis + 1, here]
            sine = phases[2 * axis + 1 : 2 * axis + 2, here]
            rc, rs, ic, is_ = real * cosine, real * sine, imag * cosine, imag * sine
            at = (1 + 2 * axis) * total
            turned[0, at : at + total, here] = (rc - is_).astype(bf16)
            turned[1, at : at + total, here] = (rs + ic).astype(bf16)
            at = at + total
            turned[0, at : at + total, here] = (rc + is_).astype(bf16)
            turned[1, at : at + total, here] = (ic - rs).astype(bf16)
    across = (((1,), (1,)), ((), ()))
    images = aligned[:, :, 0:width].reshape(2 * rows * count, width)
    real = lax.dot_general(images, turned[0], across, preferred_element_type=f32)
    imag = lax.dot_general(images, turned[1], across, preferred_element_type=f32)
    table = ctf[...].astype(f32)
    energy = lax.dot_general(
        table * table, power[...], across, precision=highest, preferred_element_type=f32
    )
    energy = jnp.concatenate([energy] * SHIFTS, axis=1) * 0.5
    for at in range(count):
        low = 2 * rows * at
        mine = slice(at * rows, (at + 1) * rows)
        dense[mine, :] = real[low : low + rows, :] + imag[low + rows : low + 2 * rows, :]
        notes[mine, :] = aligned[at, 0:rows, width : width + LANES].astype(f32)
    facts = notes[...]
    values = dense[...]
    for g in range(table.shape[0]):
        values = values - jnp.where(
            facts[:, route_count : route_count + 1] == float(g), energy[g : g + 1, :], 0.0
        )
    first = values.astype(bf16)
    rest = values - first.astype(f32)
    second = rest.astype(bf16)
    third = (rest - second.astype(f32)).astype(bf16)
    terms = [first.astype(f32), second.astype(f32), third.astype(f32)]
    direction, spot = lane_facts(total, owners, same_core, columns, place[1])
    spots = SHIFTS * held * columns
    choose = spot_table(spot, spots)
    height = out.shape[0]
    for r in range(route_count):
        listed = facts[:, r : r + 1] == direction
        chosen = jnp.zeros((rows * count, spots), f32)
        for term in terms:
            chosen = chosen + lax.dot_general(
                jnp.where(listed, term, 0.0).astype(bf16),
                choose,
                across,
                preferred_element_type=f32,
            )
        for block in range(rows * count // height):
            low = (block * route_count + r) * spots
            out[:, low : low + spots] = chosen[block * height : (block + 1) * height]


def sums_kernel(rows, route_count, columns, scores, aligned, phases, place, *outs_and_scratch):
    *outs, evidence, tall, wide = outs_and_scratch
    width = phases.shape[1]
    count = aligned.shape[0]
    cores = len(outs)
    same_core = outs[0].shape[1]
    owners = cores * same_core
    held = outs[0].shape[0] // 2
    total = held * owners
    height = scores.shape[0]
    blocks = count // (2 * height)
    listings = scores.shape[1] // blocks
    for block in range(blocks):
        tall[block * height : (block + 1) * height, :] = scores[
            :, block * listings : (block + 1) * listings
        ]
    for part in range(count // (2 * rows)):
        values = tall[part * rows : (part + 1) * rows, :]
        at = 2 * rows * part
        wide[at : at + rows, :] = values
        wide[at + rows : at + 2 * rows, :] = values
    values = wide[...]
    peak = jnp.max(values, axis=1, keepdims=True)
    mass = jnp.sum(jnp.exp(values - peak), axis=1, keepdims=True)
    log_evidence = peak + jnp.log(mass)
    evidence[...] = jnp.broadcast_to(log_evidence, evidence.shape)
    listed_weights = jnp.exp(values - log_evidence).astype(bf16)
    notes = aligned[:, width : width + LANES].astype(f32)
    direction, spot = lane_facts(total, owners, same_core, columns, place[1])
    spots = listings // route_count
    spread = spot_table(spot, spots)
    weights = jnp.zeros((count, SHIFTS * total), f32)
    for r in range(route_count):
        placed = jnp.dot(
            listed_weights[:, r * spots : (r + 1) * spots], spread, preferred_element_type=f32
        )
        weights = jnp.where(notes[:, r : r + 1] == direction, placed, weights)
    row = lax.broadcasted_iota(jnp.int32, (count, 1), 0)
    first_half = jnp.zeros((count, 1), jnp.bool_)
    for part in range(count // (2 * rows)):
        at = 2 * rows * part
        first_half = first_half | ((row >= at) & (row < at + rows))
    weights_real = jnp.where(first_half, weights, 0.0).T.astype(bf16)
    weights_imag = jnp.where(first_half, 0.0, weights).T.astype(bf16)
    chunk = 2 * LANES
    for low in range(0, width, chunk):
        high = min(low + chunk, width)
        images = aligned[:, low:high]
        real = jnp.dot(weights_real, images, preferred_element_type=f32)
        imag = jnp.dot(weights_imag, images, preferred_element_type=f32)
        u = [real[t * total : (t + 1) * total] for t in range(SHIFTS)]
        v = [imag[t * total : (t + 1) * total] for t in range(SHIFTS)]
        first, second = u[0], v[0]
        for axis in range(2):
            cosine = phases[2 * axis : 2 * axis + 1, low:high]
            sine = phases[2 * axis + 1 : 2 * axis + 2, low:high]
            one, two = 1 + 2 * axis, 2 + 2 * axis
            first = first + (u[one] + u[two]) * cosine + (v[one] - v[two]) * sine
            second = second + (v[one] + v[two]) * cosine - (u[one] - u[two]) * sine
        for k in range(held):
            for step, out in enumerate(outs):
                start = k * owners + step * same_core
                mine = slice(start, start + same_core)
                out[k, :, low:high] = first[mine].astype(out.dtype)
                out[held + k, :, low:high] = second[mine].astype(out.dtype)


def expectation(particles, projections, ctf, defocus_group, offsets, routes):
    pixel_count = KX * KY
    rows = particles.shape[0]
    route_count = routes.shape[1]
    held = projections.shape[0] * projections.shape[1]
    far, near, cores, columns = (
        lax.axis_size(name) for name in ("far", "near", "core", "cls")
    )
    group = ("near", "cls")
    same_core = ("far", "near", "cls")
    pieces = near * columns
    peers = far * pieces
    owners = peers * cores
    width = -(-pixel_count // (pieces * LANES)) * LANES
    padded = pieces * width
    place = lax.axis_index(group)
    total = held * owners
    params = pltpu.CompilerParams(vmem_limit_bytes=min(60 << 20, (8 << 20) + total * (88 << 10)))

    steps = [0] + sorted(range(1, pieces), key=exchange_order)
    where = jnp.stack([place, lax.axis_index("core")])
    scalars = pl.BlockSpec(memory_space=pltpu.SMEM)
    vectors = pl.BlockSpec(memory_space=pltpu.VMEM)
    distant = (
        projections.reshape(held, 2 * pixel_count),
        particles,
        ctf,
        defocus_group[None, :],
        offsets.T,
        routes.T,
    )
    piece = jax.ShapeDtypeStruct((2 * rows, width + LANES), bf16)
    refs, *parts = pl.pallas_call(
        functools.partial(prepare_kernel, pixel_count, width, steps),
        out_shape=[jax.ShapeDtypeStruct((peers, 2 * held, width), bf16)] + [piece] * pieces,
        in_specs=[pl.BlockSpec(memory_space=pltpu.HBM)] * len(distant) + [scalars],
        scratch_shapes=[pltpu.VMEM(array.shape, array.dtype) for array in distant]
        + [
            pltpu.VMEM((rows, pixel_count), f32),
            pltpu.VMEM((pieces, 2 * rows, width), bf16),
            pltpu.VMEM((-(-(3 + route_count) // 8) * 8, -(-rows // LANES) * LANES), f32),
            pltpu.SemaphoreType.DMA((len(distant),)),
        ],
        compiler_params=pltpu.CompilerParams(vmem_limit_bytes=60 << 20),
        name="prepare",
    )(*distant, where)
    refs = lax.all_to_all(refs, same_core, split_axis=0, concat_axis=0, tiled=True)
    blocks = [refs] + [lax.ppermute(refs, "core", routes_of(step, cores)) for step in range(1, cores)]
    blocks = [block.transpose(1, 0, 2) for block in blocks]
    parts = list(parts)
    for at in range(1, pieces):
        parts[at] = lax.ppermute(parts[at], group, routes_of(steps[at], pieces))

    column = place * width + jnp.arange(width, dtype=jnp.int32)
    across, down = column // KY, column % KY - KY // 2
    angles = jnp.stack([across, down]).astype(f32) * (2.0 * math.pi / BOX)
    phases = jnp.stack([jnp.cos(angles), jnp.sin(angles)], axis=1).reshape(4, width)
    ctf_here = lax.dynamic_slice_in_dim(
        jnp.pad(ctf, ((0, 0), (0, padded - pixel_count))), place * width, width, 1
    )

    count = pieces * rows
    listings = route_count * SHIFTS * held * columns
    folds = 4 if count % 32 == 0 else 1
    scores, aligned = pl.pallas_call(
        functools.partial(score_kernel, rows, route_count, columns, steps),
        out_shape=(
            jax.ShapeDtypeStruct((count // folds, folds * listings), f32),
            jax.ShapeDtypeStruct((pieces, 2 * rows, width + LANES), bf16),
        ),
        in_specs=[vectors] * (pieces + cores + 2) + [scalars],
        scratch_shapes=[
            pltpu.VMEM((2, SHIFTS * total, width), bf16),
            pltpu.VMEM((total, width), f32),
            pltpu.VMEM((count, SHIFTS * total), f32),
            pltpu.VMEM((count, LANES), f32),
        ],
        compiler_params=params,
        name="score",
    )(*parts, *blocks, ctf_here, phases, where)
    aligned = aligned.reshape(pieces * 2 * rows, width + LANES)

    span = 1
    while span < pieces:
        scores = scores + lax.ppermute(scores, group, [(i, i ^ span) for i in range(pieces)])
        span *= 2

    kinds = [f32] + [bf16] * (cores - 1)
    *sums, evidence = pl.pallas_call(
        functools.partial(sums_kernel, rows, route_count, columns),
        out_shape=(
            *(jax.ShapeDtypeStruct((2 * held, peers, width), kind) for kind in kinds),
            jax.ShapeDtypeStruct((2 * pieces * rows, LANES), f32),
        ),
        in_specs=[vectors] * 3 + [scalars],
        scratch_shapes=[pltpu.VMEM((count, listings), f32), pltpu.VMEM((2 * count, listings), f32)],
        compiler_params=params,
        name="sums",
    )(scores, aligned, phases, where)
    log_evidence = lax.dynamic_slice_in_dim(evidence, place * 2 * rows, rows, 0)[:, 0]

    merged = sums[0]
    for step in range(1, cores):
        merged = merged + lax.ppermute(sums[step], "core", routes_of(step, cores)).astype(f32)
    merged = merged.astype(bf16).transpose(1, 0, 2)
    merged = lax.all_to_all(merged, same_core, split_axis=0, concat_axis=0, tiled=True)
    data_sum = jnp.sum(merged.reshape(far, pieces, 2 * held, width).astype(f32), axis=0)
    data_sum = data_sum.astype(bf16).reshape(pieces, 2, held, width).transpose(2, 1, 0, 3)
    data_sum = data_sum.reshape(held, 2, padded)[:, :, :pixel_count]
    return (log_evidence, data_sum.reshape(projections.shape))


def solution(mesh):
    groups, orient, columns = (mesh.shape[name] for name in ("groups", "orient", "cls"))
    cores = 2 if orient % 2 == 0 else 1
    near = 2 if orient % (2 * cores) == 0 else 1
    axes = ("groups", "far", "near", "core", "cls")
    along = ("far", "near", "core")
    inner = Mesh(
        mesh.devices.reshape(groups, orient // (near * cores), near, cores, columns), axes
    )
    placed = (
        P(axes, None),
        P("cls", along, None),
        P(),
        P(axes),
        P(axes, None),
        P(axes, None),
    )
    return jax.shard_map(
        expectation,
        mesh=inner,
        in_specs=placed,
        out_specs=(P(axes), P(("groups", "cls"), along, None)),
        check_vma=False,
    )
```

```python
import functools
import math

import jax
import jax.numpy as jnp
from jax import lax
from jax.experimental import pallas as pl
from jax.experimental.pallas import tpu as pltpu
from jax.sharding import Mesh
from jax.sharding import PartitionSpec as P


KX = 86
KY = 192
BOX = 256
LANES = 128
SHIFTS = 5

highest = lax.Precision.HIGHEST
f32 = jnp.float32
bf16 = jnp.bfloat16


def unit_circle(turns):
    quarter = BOX // 4
    quadrant = jnp.floor(turns * (1.0 / quarter) + 0.5)
    angle = (turns - quadrant * quarter) * (2.0 * math.pi / BOX)
    quadrant = quadrant - 4.0 * jnp.floor(quadrant * 0.25)
    square = angle * angle
    sine = angle * (
        1.0
        + square
        * (-1.0 / 6 + square * (1.0 / 120 + square * (-1.0 / 5040 + square * (1.0 / 362880))))
    )
    cosine = 1.0 + square * (
        -0.5 + square * (1.0 / 24 + square * (-1.0 / 720 + square * (1.0 / 40320)))
    )
    odd = (quadrant == 1.0) | (quadrant == 3.0)
    first = jnp.where(odd, sine, cosine)
    second = jnp.where(odd, cosine, sine)
    first = jnp.where((quadrant == 1.0) | (quadrant == 2.0), -first, first)
    second = jnp.where(quadrant >= 2.0, -second, second)
    return first, second


def other(place, step, size):
    if size & (size - 1) == 0:
        return place ^ step
    return lax.rem(place + step, size)


def source(place, step, size):
    if size & (size - 1) == 0:
        return place ^ step
    return lax.rem(place + size - step, size)


def exchange_order(step):
    return (step.bit_count() == 2, -step.bit_count(), step)


def routes_of(step, size):
    return [(i, int(other(i, step, size))) for i in range(size)]


def split_refs(pixel_count, width, refs, out):
    held = refs.shape[0]
    pieces = -(-pixel_count // width)
    for piece in range(pieces):
        low = piece * width
        size = min(width, pixel_count - low)
        for half in range(2):
            values = refs[:, half * pixel_count + low : half * pixel_count + low + size]
            for copy in range(piece, out.shape[0], pieces):
                out[copy, half * held : (half + 1) * held, 0:size] = values
                if size < width:
                    out[copy, half * held : (half + 1) * held, size:width] = jnp.zeros(
                        (held, width - size), bf16
                    )


def prepare_kernel(pixel_count, width, steps, *refs):
    distant, (place, split), rest = refs[:6], refs[6:8], refs[8:]
    outs, near, (ctf_rows, whole, table, arrived) = rest[: len(steps)], rest[len(steps) : -4], rest[-4:]
    copies = [
        pltpu.make_async_copy(far, here, arrived.at[i])
        for i, (far, here) in enumerate(zip(distant, near))
    ]
    for copy in copies:
        copy.start()
    copies[0].wait()
    split_refs(pixel_count, width, near[0], split)
    for copy in copies[1:]:
        copy.wait()
    align(pixel_count, width, steps, *near[1:], place, outs, ctf_rows, whole, table)


def align(
    pixel_count, width, steps, images, ctf, groups, offsets, routes, place, outs, ctf_rows, whole, table
):
    rows = images.shape[0]
    pieces = len(outs)
    route_count = routes.shape[0]
    table[...] = jnp.zeros(table.shape, f32)
    table[0:2, 0:rows] = offsets[...].astype(f32)
    table[2:3, 0:rows] = groups[...].astype(f32)
    table[3 : 3 + route_count, 0:rows] = routes[...].astype(f32)
    facts = table[...].T[0:rows]
    shift_across, shift_down, group = facts[:, 0:1], facts[:, 1:2], facts[:, 2:3]
    block = math.lcm(LANES, KY)
    per_block = block // LANES
    onehot = (
        group == lax.broadcasted_iota(jnp.int32, (rows, ctf.shape[0]), 1).astype(f32)
    ).astype(bf16)
    ctf_rows[...] = jnp.dot(onehot, ctf[...], preferred_element_type=f32)
    lane = lax.broadcasted_iota(jnp.int32, (rows, block), 1)
    across = jnp.zeros((rows, block), jnp.int32)
    for step in range(1, block // KY):
        across = across + (lane >= step * KY).astype(jnp.int32)
    down = lane - across * KY - KY // 2
    base_cos, base_sin = unit_circle(
        across.astype(f32) * shift_across + down.astype(f32) * shift_down
    )
    blocks = -(-pixel_count // block)
    start = lax.broadcasted_iota(jnp.int32, (rows, blocks), 1) * (block // KY)
    start_cos, start_sin = unit_circle(start.astype(f32) * shift_across)
    for piece in range(pieces):
        for part in range(width // LANES):
            low = piece * width + part * LANES
            here = slice(part * LANES, (part + 1) * LANES)
            if low >= pixel_count:
                whole[piece, :, here] = jnp.zeros((2 * rows, LANES), bf16)
                continue
            turn, step = divmod(low // LANES, per_block)
            bc = base_cos[:, step * LANES : (step + 1) * LANES]
            bs = base_sin[:, step * LANES : (step + 1) * LANES]
            rc = start_cos[:, turn : turn + 1]
            rs = start_sin[:, turn : turn + 1]
            cosine = bc * rc - bs * rs
            sine = bs * rc + bc * rs
            scale = ctf_rows[:, low : low + LANES]
            real = images[:, low : low + LANES].astype(f32)
            imag = images[:, pixel_count + low : pixel_count + low + LANES].astype(f32)
            first = (real * cosine + imag * sine) * scale
            second = (imag * cosine - real * sine) * scale
            whole[piece, :, here] = jnp.concatenate([first, second], axis=0).astype(bf16)
    lane = lax.broadcasted_iota(jnp.int32, (rows, LANES), 1)
    notes = jnp.where(lane == route_count, group, 0.0)
    for r in range(route_count):
        notes = jnp.where(lane == r, facts[:, 3 + r : 4 + r], notes)
    notes = jnp.concatenate([notes, notes], axis=0).astype(bf16)
    for step, out in zip(steps, outs):
        out[:, 0:width] = whole[other(place[0], step, pieces)]
        out[:, width : width + LANES] = notes


def lane_facts(total, owners, same_core, columns, core_here):
    lane = lax.broadcasted_iota(jnp.int32, (1, SHIFTS * total), 1)
    owner = lax.rem(lane, owners)
    core = source(core_here, owner // same_core, owners // same_core)
    direction = (lax.rem(owner, same_core) // columns) * (owners // same_core) + core
    shift, held = lane // total, lax.rem(lane, total) // owners
    spot = (shift * (total // owners) + held) * columns + lax.rem(owner, columns)
    return direction.astype(f32), spot.astype(f32)


def spot_table(spot, spots):
    row = lax.broadcasted_iota(jnp.int32, (spots, spot.shape[1]), 0).astype(f32)
    return jnp.where(row == spot, 1.0, 0.0).astype(bf16)


def score_kernel(rows, route_count, columns, steps, *refs_all):
    count = len(steps)
    parts = refs_all[:count]
    *blocks, ctf, phases, place, out, aligned, turned, power, dense, notes, packed = (
        refs_all[count:]
    )
    same_core = blocks[0].shape[1]
    owners = len(blocks) * same_core
    width = phases.shape[1]
    held = blocks[0].shape[0] // 2
    total = held * len(blocks) * blocks[0].shape[1]
    for step, part in zip(steps, parts):
        aligned[source(place[0], step, count)] = part[...]
    for low in range(0, width, LANES):
        here = slice(low, low + LANES)
        real = jnp.concatenate(
            [block[k, :, here] for k in range(held) for block in blocks], axis=0
        )
        imag = jnp.concatenate(
            [block[held + k, :, here] for k in range(held) for block in blocks], axis=0
        )
        turned[0, 0:total, here] = real
        turned[1, 0:total, here] = imag
        real, imag = real.astype(f32), imag.astype(f32)
        power[:, here] = real * real + imag * imag
        for axis in range(2):
            cosine = phases[2 * axis : 2 * axis + 1, here]
            sine = phases[2 * axis + 1 : 2 * axis + 2, here]
            rc, rs, ic, is_ = real * cosine, real * sine, imag * cosine, imag * sine
            at = (1 + 2 * axis) * total
            turned[0, at : at + total, here] = (rc - is_).astype(bf16)
            turned[1, at : at + total, here] = (rs + ic).astype(bf16)
            at = at + total
            turned[0, at : at + total, here] = (rc + is_).astype(bf16)
            turned[1, at : at + total, here] = (ic - rs).astype(bf16)
    across = (((1,), (1,)), ((), ()))
    images = aligned[:, :, 0:width].reshape(2 * rows * count, width)
    real = lax.dot_general(images, turned[0], across, preferred_element_type=f32)
    imag = lax.dot_general(images, turned[1], across, preferred_element_type=f32)
    table = ctf[...].astype(f32)
    energy = lax.dot_general(
        table * table, power[...], across, precision=highest, preferred_element_type=f32
    )
    energy = jnp.concatenate([energy] * SHIFTS, axis=1) * 0.5
    for at in range(count):
        low = 2 * rows * at
        mine = slice(at * rows, (at + 1) * rows)
        dense[mine, :] = real[low : low + rows, :] + imag[low + rows : low + 2 * rows, :]
        notes[mine, :] = aligned[at, 0:rows, width : width + LANES].astype(f32)
    facts = notes[...]
    values = dense[...]
    for g in range(table.shape[0]):
        values = values - jnp.where(
            facts[:, route_count : route_count + 1] == float(g), energy[g : g + 1, :], 0.0
        )
    first = values.astype(bf16)
    rest = values - first.astype(f32)
    second = rest.astype(bf16)
    third = (rest - second.astype(f32)).astype(bf16)
    terms = [first.astype(f32), second.astype(f32), third.astype(f32)]
    direction, spot = lane_facts(total, owners, same_core, columns, place[1])
    spots = SHIFTS * held * columns
    particles = rows * count
    stacked = []
    for r in range(route_count):
        listed = facts[:, r : r + 1] == direction
        stacked += [jnp.where(listed, term, 0.0).astype(bf16) for term in terms]
    chosen = lax.dot_general(
        jnp.concatenate(stacked, axis=0),
        spot_table(spot, spots),
        across,
        preferred_element_type=f32,
    )
    height = out.shape[1]
    for r in range(route_count):
        low = r * len(terms) * particles
        mine = chosen[low : low + particles]
        for term in range(1, len(terms)):
            mine = mine + chosen[low + term * particles : low + (term + 1) * particles]
        for block in range(particles // height):
            at = (block * route_count + r) * spots
            packed[:, at : at + spots] = mine[block * height : (block + 1) * height]
    for copy in range(out.shape[0]):
        out[copy] = packed[...]


def sums_kernel(rows, route_count, columns, scores, aligned, phases, place, *outs_and_scratch):
    *outs, evidence, tall, wide = outs_and_scratch
    width = phases.shape[1]
    count = aligned.shape[0]
    cores = len(outs)
    same_core = outs[0].shape[1]
    owners = cores * same_core
    held = outs[0].shape[0] // 2
    total = held * owners
    height = scores.shape[1]
    blocks = count // (2 * height)
    listings = scores.shape[2] // blocks
    summed = scores[0]
    for part in range(1, scores.shape[0]):
        summed = summed + scores[part]
    for block in range(blocks):
        tall[block * height : (block + 1) * height, :] = summed[
            :, block * listings : (block + 1) * listings
        ]
    for part in range(count // (2 * rows)):
        values = tall[part * rows : (part + 1) * rows, :]
        at = 2 * rows * part
        wide[at : at + rows, :] = values
        wide[at + rows : at + 2 * rows, :] = values
    values = wide[...]
    peak = jnp.max(values, axis=1, keepdims=True)
    mass = jnp.sum(jnp.exp(values - peak), axis=1, keepdims=True)
    log_evidence = peak + jnp.log(mass)
    evidence[...] = jnp.broadcast_to(log_evidence, evidence.shape)
    listed_weights = jnp.exp(values - log_evidence).astype(bf16)
    notes = aligned[:, width : width + LANES].astype(f32)
    direction, spot = lane_facts(total, owners, same_core, columns, place[1])
    spots = listings // route_count
    spread = spot_table(spot, spots)
    weights = jnp.zeros((count, SHIFTS * total), f32)
    for r in range(route_count):
        placed = jnp.dot(
            listed_weights[:, r * spots : (r + 1) * spots], spread, preferred_element_type=f32
        )
        weights = jnp.where(notes[:, r : r + 1] == direction, placed, weights)
    row = lax.broadcasted_iota(jnp.int32, (count, 1), 0)
    first_half = jnp.zeros((count, 1), jnp.bool_)
    for part in range(count // (2 * rows)):
        at = 2 * rows * part
        first_half = first_half | ((row >= at) & (row < at + rows))
    weights_real = jnp.where(first_half, weights, 0.0).T.astype(bf16)
    weights_imag = jnp.where(first_half, 0.0, weights).T.astype(bf16)
    chunk = 2 * LANES
    for low in range(0, width, chunk):
        high = min(low + chunk, width)
        images = aligned[:, low:high]
        real = jnp.dot(weights_real, images, preferred_element_type=f32)
        imag = jnp.dot(weights_imag, images, preferred_element_type=f32)
        u = [real[t * total : (t + 1) * total] for t in range(SHIFTS)]
        v = [imag[t * total : (t + 1) * total] for t in range(SHIFTS)]
        first, second = u[0], v[0]
        for axis in range(2):
            cosine = phases[2 * axis : 2 * axis + 1, low:high]
            sine = phases[2 * axis + 1 : 2 * axis + 2, low:high]
            one, two = 1 + 2 * axis, 2 + 2 * axis
            first = first + (u[one] + u[two]) * cosine + (v[one] - v[two]) * sine
            second = second + (v[one] + v[two]) * cosine - (u[one] - u[two]) * sine
        for k in range(held):
            for step, out in enumerate(outs):
                start = k * owners + step * same_core
                mine = slice(start, start + same_core)
                out[k, :, low:high] = first[mine].astype(out.dtype)
                out[held + k, :, low:high] = second[mine].astype(out.dtype)


def expectation(particles, projections, ctf, defocus_group, offsets, routes):
    pixel_count = KX * KY
    rows = particles.shape[0]
    route_count = routes.shape[1]
    held = projections.shape[0] * projections.shape[1]
    far, near, cores, columns = (
        lax.axis_size(name) for name in ("far", "near", "core", "cls")
    )
    group = ("near", "cls")
    same_core = ("far", "near", "cls")
    pieces = near * columns
    peers = far * pieces
    owners = peers * cores
    width = -(-pixel_count // (pieces * LANES)) * LANES
    padded = pieces * width
    place = lax.axis_index(group)
    total = held * owners
    params = pltpu.CompilerParams(vmem_limit_bytes=min(60 << 20, (8 << 20) + total * (88 << 10)))

    steps = [0] + sorted(range(1, pieces), key=exchange_order)
    where = jnp.stack([place, lax.axis_index("core")])
    scalars = pl.BlockSpec(memory_space=pltpu.SMEM)
    vectors = pl.BlockSpec(memory_space=pltpu.VMEM)
    distant = (
        projections.reshape(held, 2 * pixel_count),
        particles,
        ctf,
        defocus_group[None, :],
        offsets.T,
        routes.T,
    )
    piece = jax.ShapeDtypeStruct((2 * rows, width + LANES), bf16)
    refs, *parts = pl.pallas_call(
        functools.partial(prepare_kernel, pixel_count, width, steps),
        out_shape=[jax.ShapeDtypeStruct((peers, 2 * held, width), bf16)] + [piece] * pieces,
        in_specs=[pl.BlockSpec(memory_space=pltpu.HBM)] * len(distant) + [scalars],
        scratch_shapes=[pltpu.VMEM(array.shape, array.dtype) for array in distant]
        + [
            pltpu.VMEM((rows, pixel_count), f32),
            pltpu.VMEM((pieces, 2 * rows, width), bf16),
            pltpu.VMEM((-(-(3 + route_count) // 8) * 8, -(-rows // LANES) * LANES), f32),
            pltpu.SemaphoreType.DMA((len(distant),)),
        ],
        compiler_params=pltpu.CompilerParams(vmem_limit_bytes=60 << 20),
        name="prepare",
    )(*distant, where)
    refs = lax.all_to_all(refs, same_core, split_axis=0, concat_axis=0, tiled=True)
    blocks = [refs] + [lax.ppermute(refs, "core", routes_of(step, cores)) for step in range(1, cores)]
    blocks = [block.transpose(1, 0, 2) for block in blocks]
    parts = list(parts)
    for at in range(1, pieces):
        parts[at] = lax.ppermute(parts[at], group, routes_of(steps[at], pieces))

    column = place * width + jnp.arange(width, dtype=jnp.int32)
    across, down = column // KY, column % KY - KY // 2
    angles = jnp.stack([across, down]).astype(f32) * (2.0 * math.pi / BOX)
    phases = jnp.stack([jnp.cos(angles), jnp.sin(angles)], axis=1).reshape(4, width)
    ctf_here = lax.dynamic_slice_in_dim(
        jnp.pad(ctf, ((0, 0), (0, padded - pixel_count))), place * width, width, 1
    )

    count = pieces * rows
    listings = route_count * SHIFTS * held * columns
    folds = 4 if count % 32 == 0 else 1
    scores, aligned = pl.pallas_call(
        functools.partial(score_kernel, rows, route_count, columns, steps),
        out_shape=(
            jax.ShapeDtypeStruct((pieces, count // folds, folds * listings), f32),
            jax.ShapeDtypeStruct((pieces, 2 * rows, width + LANES), bf16),
        ),
        in_specs=[vectors] * (pieces + cores + 2) + [scalars],
        scratch_shapes=[
            pltpu.VMEM((2, SHIFTS * total, width), bf16),
            pltpu.VMEM((total, width), f32),
            pltpu.VMEM((count, SHIFTS * total), f32),
            pltpu.VMEM((count, LANES), f32),
            pltpu.VMEM((count // folds, folds * listings), f32),
        ],
        compiler_params=params,
        name="score",
    )(*parts, *blocks, ctf_here, phases, where)
    aligned = aligned.reshape(pieces * 2 * rows, width + LANES)

    scores = lax.all_to_all(scores, group, split_axis=0, concat_axis=0, tiled=True)

    kinds = [f32] + [bf16] * (cores - 1)
    *sums, evidence = pl.pallas_call(
        functools.partial(sums_kernel, rows, route_count, columns),
        out_shape=(
            *(jax.ShapeDtypeStruct((2 * held, peers, width), kind) for kind in kinds),
            jax.ShapeDtypeStruct((2 * pieces * rows, LANES), f32),
        ),
        in_specs=[vectors] * 3 + [scalars],
        scratch_shapes=[pltpu.VMEM((count, listings), f32), pltpu.VMEM((2 * count, listings), f32)],
        compiler_params=params,
        name="sums",
    )(scores, aligned, phases, where)
    log_evidence = lax.dynamic_slice_in_dim(evidence, place * 2 * rows, rows, 0)[:, 0]

    merged = sums[0]
    for step in range(1, cores):
        merged = merged + lax.ppermute(sums[step], "core", routes_of(step, cores)).astype(f32)
    merged = merged.astype(bf16).transpose(1, 0, 2)
    merged = lax.all_to_all(merged, same_core, split_axis=0, concat_axis=0, tiled=True)
    data_sum = jnp.sum(merged.reshape(far, pieces, 2 * held, width).astype(f32), axis=0)
    data_sum = data_sum.astype(bf16).reshape(pieces, 2, held, width).transpose(2, 1, 0, 3)
    data_sum = data_sum.reshape(held, 2, padded)[:, :, :pixel_count]
    return (log_evidence, data_sum.reshape(projections.shape))


def solution(mesh):
    groups, orient, columns = (mesh.shape[name] for name in ("groups", "orient", "cls"))
    cores = 2 if orient % 2 == 0 else 1
    near = 2 if orient % (2 * cores) == 0 else 1
    axes = ("groups", "far", "near", "core", "cls")
    along = ("far", "near", "core")
    inner = Mesh(
        mesh.devices.reshape(groups, orient // (near * cores), near, cores, columns), axes
    )
    placed = (
        P(axes, None),
        P("cls", along, None),
        P(),
        P(axes),
        P(axes, None),
        P(axes, None),
    )
    return jax.shard_map(
        expectation,
        mesh=inner,
        in_specs=placed,
        out_specs=(P(axes), P(("groups", "cls"), along, None)),
        check_vma=False,
    )
```

```python
import functools
import math

import jax
import jax.numpy as jnp
from jax import lax
from jax.experimental import pallas as pl
from jax.experimental.pallas import tpu as pltpu
from jax.sharding import Mesh
from jax.sharding import PartitionSpec as P


KX = 86
KY = 192
BOX = 256
LANES = 128
SHIFTS = 5

highest = lax.Precision.HIGHEST
f32 = jnp.float32
bf16 = jnp.bfloat16


def unit_circle(turns):
    quarter = BOX // 4
    quadrant = jnp.floor(turns * (1.0 / quarter) + 0.5)
    angle = (turns - quadrant * quarter) * (2.0 * math.pi / BOX)
    quadrant = quadrant - 4.0 * jnp.floor(quadrant * 0.25)
    square = angle * angle
    sine = angle * (
        1.0
        + square
        * (-1.0 / 6 + square * (1.0 / 120 + square * (-1.0 / 5040 + square * (1.0 / 362880))))
    )
    cosine = 1.0 + square * (
        -0.5 + square * (1.0 / 24 + square * (-1.0 / 720 + square * (1.0 / 40320)))
    )
    odd = (quadrant == 1.0) | (quadrant == 3.0)
    first = jnp.where(odd, sine, cosine)
    second = jnp.where(odd, cosine, sine)
    first = jnp.where((quadrant == 1.0) | (quadrant == 2.0), -first, first)
    second = jnp.where(quadrant >= 2.0, -second, second)
    return first, second


def other(place, step, size):
    if size & (size - 1) == 0:
        return place ^ step
    return lax.rem(place + step, size)


def source(place, step, size):
    if size & (size - 1) == 0:
        return place ^ step
    return lax.rem(place + size - step, size)


def exchange_order(step):
    return (step.bit_count() == 2, -step.bit_count(), step)


def routes_of(step, size):
    return [(i, int(other(i, step, size))) for i in range(size)]


def split_refs(pixel_count, width, refs, out):
    held = refs.shape[0]
    pieces = -(-pixel_count // width)
    for piece in range(pieces):
        low = piece * width
        size = min(width, pixel_count - low)
        for half in range(2):
            values = refs[:, half * pixel_count + low : half * pixel_count + low + size]
            for copy in range(piece, out.shape[0], pieces):
                out[copy, half * held : (half + 1) * held, 0:size] = values
                if size < width:
                    out[copy, half * held : (half + 1) * held, size:width] = jnp.zeros(
                        (held, width - size), bf16
                    )


def prepare_kernel(pixel_count, width, steps, group, *refs):
    distant, (split, *outs), rest = refs[:6], refs[6 : 7 + len(steps)], refs[7 + len(steps) :]
    near, (split_here, whole, ctf_rows, table, arrived, left) = rest[:6], rest[6:]
    copies = [
        pltpu.make_async_copy(far, here, arrived.at[i])
        for i, (far, here) in enumerate(zip(distant, near))
    ]
    for copy in copies:
        copy.start()
    copies[0].wait()
    split_refs(pixel_count, width, near[0], split_here)
    sent = [pltpu.make_async_copy(split_here, split, left.at[0])]
    sent[0].start()
    for copy in copies[2:]:
        copy.wait()
    align(pixel_count, width, *near[1:], whole, ctf_rows, table, copies[1])
    place = lax.axis_index(group)
    for step, out in zip(steps, outs):
        piece = whole.at[other(place, step, len(steps))]
        sent.append(pltpu.make_async_copy(piece, out, left.at[len(sent)]))
        sent[-1].start()
    for copy in sent:
        copy.wait()


def align(
    pixel_count, width, images, ctf, groups, offsets, routes, whole, ctf_rows, table, coming
):
    rows = images.shape[0]
    pieces = whole.shape[0]
    route_count = routes.shape[0]
    table[...] = jnp.zeros(table.shape, f32)
    table[0:2, 0:rows] = offsets[...].astype(f32)
    table[2:3, 0:rows] = groups[...].astype(f32)
    table[3 : 3 + route_count, 0:rows] = routes[...].astype(f32)
    facts = table[...].T[0:rows]
    shift_across, shift_down, group = facts[:, 0:1], facts[:, 1:2], facts[:, 2:3]
    block = math.lcm(LANES, KY)
    per_block = block // LANES
    onehot = (
        group == lax.broadcasted_iota(jnp.int32, (rows, ctf.shape[0]), 1).astype(f32)
    ).astype(bf16)
    ctf_rows[...] = jnp.dot(onehot, ctf[...], preferred_element_type=f32)
    lane = lax.broadcasted_iota(jnp.int32, (rows, block), 1)
    across = jnp.zeros((rows, block), jnp.int32)
    for step in range(1, block // KY):
        across = across + (lane >= step * KY).astype(jnp.int32)
    down = lane - across * KY - KY // 2
    base_cos, base_sin = unit_circle(
        across.astype(f32) * shift_across + down.astype(f32) * shift_down
    )
    blocks = -(-pixel_count // block)
    start = lax.broadcasted_iota(jnp.int32, (rows, blocks), 1) * (block // KY)
    start_cos, start_sin = unit_circle(start.astype(f32) * shift_across)
    coming.wait()
    for piece in range(pieces):
        for part in range(width // LANES):
            low = piece * width + part * LANES
            here = slice(part * LANES, (part + 1) * LANES)
            if low >= pixel_count:
                whole[piece, :, here] = jnp.zeros((2 * rows, LANES), bf16)
                continue
            turn, step = divmod(low // LANES, per_block)
            bc = base_cos[:, step * LANES : (step + 1) * LANES]
            bs = base_sin[:, step * LANES : (step + 1) * LANES]
            rc = start_cos[:, turn : turn + 1]
            rs = start_sin[:, turn : turn + 1]
            cosine = bc * rc - bs * rs
            sine = bs * rc + bc * rs
            scale = ctf_rows[:, low : low + LANES]
            real = images[:, low : low + LANES].astype(f32)
            imag = images[:, pixel_count + low : pixel_count + low + LANES].astype(f32)
            first = (real * cosine + imag * sine) * scale
            second = (imag * cosine - real * sine) * scale
            whole[piece, :, here] = jnp.concatenate([first, second], axis=0).astype(bf16)
    lane = lax.broadcasted_iota(jnp.int32, (rows, LANES), 1)
    notes = jnp.where(lane == route_count, group, 0.0)
    for r in range(route_count):
        notes = jnp.where(lane == r, facts[:, 3 + r : 4 + r], notes)
    notes = jnp.concatenate([notes, notes], axis=0).astype(bf16)
    for piece in range(pieces):
        whole[piece, :, width : width + LANES] = notes


def lane_facts(total, owners, same_core, columns, core_here):
    lane = lax.broadcasted_iota(jnp.int32, (1, SHIFTS * total), 1)
    owner = lax.rem(lane, owners)
    core = source(core_here, owner // same_core, owners // same_core)
    direction = (lax.rem(owner, same_core) // columns) * (owners // same_core) + core
    shift, held = lane // total, lax.rem(lane, total) // owners
    spot = (shift * (total // owners) + held) * columns + lax.rem(owner, columns)
    return direction.astype(f32), spot.astype(f32)


def spot_table(spot, spots):
    row = lax.broadcasted_iota(jnp.int32, (spots, spot.shape[1]), 0).astype(f32)
    return jnp.where(row == spot, 1.0, 0.0).astype(bf16)


def block_facts(held, peers, blocks, columns, core_here):
    each = SHIFTS * held * peers
    lane = lax.broadcasted_iota(jnp.int32, (1, each * blocks), 1)
    inside, peer = lax.rem(lane, each), lax.rem(lane, peers)
    core = source(core_here, lane // each, blocks)
    direction = (peer // columns) * blocks + core
    spot = (inside // peers) * columns + lax.rem(peer, columns)
    return direction.astype(f32), spot.astype(f32)


def turn_kernel(refs, ctf, phases, turned, energy, power):
    width = phases.shape[1]
    held = refs.shape[0] // 2
    total = held * refs.shape[1]
    for low in range(0, width, LANES):
        here = slice(low, low + LANES)
        real = jnp.concatenate([refs[k, :, here] for k in range(held)], axis=0)
        imag = jnp.concatenate([refs[held + k, :, here] for k in range(held)], axis=0)
        turned[0, 0:total, here] = real
        turned[1, 0:total, here] = imag
        real, imag = real.astype(f32), imag.astype(f32)
        power[:, here] = real * real + imag * imag
        for axis in range(2):
            cosine = phases[2 * axis : 2 * axis + 1, here]
            sine = phases[2 * axis + 1 : 2 * axis + 2, here]
            rc, rs, ic, is_ = real * cosine, real * sine, imag * cosine, imag * sine
            at = (1 + 2 * axis) * total
            turned[0, at : at + total, here] = (rc - is_).astype(bf16)
            turned[1, at : at + total, here] = (rs + ic).astype(bf16)
            at = at + total
            turned[0, at : at + total, here] = (rc + is_).astype(bf16)
            turned[1, at : at + total, here] = (ic - rs).astype(bf16)
    table = ctf[...].astype(f32)
    half = 0.5 * lax.dot_general(
        table * table,
        power[...],
        (((1,), (1,)), ((), ())),
        precision=highest,
        preferred_element_type=f32,
    )
    energy[...] = jnp.concatenate([half] * SHIFTS, axis=1)


def score_kernel(rows, route_count, columns, held, cores, steps, *refs_all):
    count = len(steps)
    parts, blocks, energies = refs_all[:count], refs_all[count:][:cores], refs_all[count + cores :][:cores]
    place, out, aligned, dense, notes, packed = refs_all[count + 2 * cores :]
    width = blocks[0].shape[2]
    each = blocks[0].shape[1]
    for step, part in zip(steps, parts):
        aligned[source(place[0], step, count)] = part[...]
    across = (((1,), (1,)), ((), ()))
    images = aligned[:, :, 0:width].reshape(2 * rows * count, width)
    for block, turned in enumerate(blocks):
        real = lax.dot_general(images, turned[0], across, preferred_element_type=f32)
        imag = lax.dot_general(images, turned[1], across, preferred_element_type=f32)
        for at in range(count):
            low = 2 * rows * at
            dense[at * rows : (at + 1) * rows, block * each : (block + 1) * each] = (
                real[low : low + rows, :] + imag[low + rows : low + 2 * rows, :]
            )
    for at in range(count):
        mine = slice(at * rows, (at + 1) * rows)
        notes[mine, :] = aligned[at, 0:rows, width : width + LANES].astype(f32)
    energy = jnp.concatenate([energy[...] for energy in energies], axis=1)
    facts = notes[...]
    values = dense[...]
    for g in range(energy.shape[0]):
        values = values - jnp.where(
            facts[:, route_count : route_count + 1] == float(g), energy[g : g + 1, :], 0.0
        )
    first = values.astype(bf16)
    rest = values - first.astype(f32)
    second = rest.astype(bf16)
    third = (rest - second.astype(f32)).astype(bf16)
    terms = [first.astype(f32), second.astype(f32), third.astype(f32)]
    direction, spot = block_facts(held, each // (SHIFTS * held), cores, columns, place[1])
    spots = SHIFTS * held * columns
    particles = rows * count
    stacked = []
    for r in range(route_count):
        listed = facts[:, r : r + 1] == direction
        stacked += [jnp.where(listed, term, 0.0).astype(bf16) for term in terms]
    chosen = lax.dot_general(
        jnp.concatenate(stacked, axis=0),
        spot_table(spot, spots),
        across,
        preferred_element_type=f32,
    )
    height = out.shape[1]
    for r in range(route_count):
        low = r * len(terms) * particles
        mine = chosen[low : low + particles]
        for term in range(1, len(terms)):
            mine = mine + chosen[low + term * particles : low + (term + 1) * particles]
        for block in range(particles // height):
            at = (block * route_count + r) * spots
            packed[:, at : at + spots] = mine[block * height : (block + 1) * height]
    for copy in range(out.shape[0]):
        out[copy] = packed[...]


def sums_kernel(rows, route_count, columns, scores, aligned, phases, place, *outs_and_scratch):
    *outs, evidence, tall, wide = outs_and_scratch
    width = phases.shape[1]
    count = aligned.shape[0]
    cores = len(outs)
    same_core = outs[0].shape[1]
    owners = cores * same_core
    held = outs[0].shape[0] // 2
    total = held * owners
    height = scores.shape[1]
    blocks = count // (2 * height)
    listings = scores.shape[2] // blocks
    summed = scores[0]
    for part in range(1, scores.shape[0]):
        summed = summed + scores[part]
    for block in range(blocks):
        tall[block * height : (block + 1) * height, :] = summed[
            :, block * listings : (block + 1) * listings
        ]
    for part in range(count // (2 * rows)):
        values = tall[part * rows : (part + 1) * rows, :]
        at = 2 * rows * part
        wide[at : at + rows, :] = values
        wide[at + rows : at + 2 * rows, :] = values
    values = wide[...]
    peak = jnp.max(values, axis=1, keepdims=True)
    mass = jnp.sum(jnp.exp(values - peak), axis=1, keepdims=True)
    log_evidence = peak + jnp.log(mass)
    evidence[...] = jnp.broadcast_to(log_evidence, evidence.shape)
    listed_weights = jnp.exp(values - log_evidence).astype(bf16)
    notes = aligned[:, width : width + LANES].astype(f32)
    direction, spot = lane_facts(total, owners, same_core, columns, place[1])
    spots = listings // route_count
    spread = spot_table(spot, spots)
    weights = jnp.zeros((count, SHIFTS * total), f32)
    for r in range(route_count):
        placed = jnp.dot(
            listed_weights[:, r * spots : (r + 1) * spots], spread, preferred_element_type=f32
        )
        weights = jnp.where(notes[:, r : r + 1] == direction, placed, weights)
    row = lax.broadcasted_iota(jnp.int32, (count, 1), 0)
    first_half = jnp.zeros((count, 1), jnp.bool_)
    for part in range(count // (2 * rows)):
        at = 2 * rows * part
        first_half = first_half | ((row >= at) & (row < at + rows))
    weights_real = jnp.where(first_half, weights, 0.0).T.astype(bf16)
    weights_imag = jnp.where(first_half, 0.0, weights).T.astype(bf16)
    chunk = 2 * LANES
    for low in range(0, width, chunk):
        high = min(low + chunk, width)
        images = aligned[:, low:high]
        real = jnp.dot(weights_real, images, preferred_element_type=f32)
        imag = jnp.dot(weights_imag, images, preferred_element_type=f32)
        u = [real[t * total : (t + 1) * total] for t in range(SHIFTS)]
        v = [imag[t * total : (t + 1) * total] for t in range(SHIFTS)]
        first, second = u[0], v[0]
        for axis in range(2):
            cosine = phases[2 * axis : 2 * axis + 1, low:high]
            sine = phases[2 * axis + 1 : 2 * axis + 2, low:high]
            one, two = 1 + 2 * axis, 2 + 2 * axis
            first = first + (u[one] + u[two]) * cosine + (v[one] - v[two]) * sine
            second = second + (v[one] + v[two]) * cosine - (u[one] - u[two]) * sine
        for k in range(held):
            for step, out in enumerate(outs):
                start = k * owners + step * same_core
                mine = slice(start, start + same_core)
                out[k, :, low:high] = first[mine].astype(out.dtype)
                out[held + k, :, low:high] = second[mine].astype(out.dtype)


def expectation(particles, projections, ctf, defocus_group, offsets, routes):
    pixel_count = KX * KY
    rows = particles.shape[0]
    route_count = routes.shape[1]
    held = projections.shape[0] * projections.shape[1]
    far, near, cores, columns = (
        lax.axis_size(name) for name in ("far", "near", "core", "cls")
    )
    group = ("near", "cls")
    same_core = ("far", "near", "cls")
    pieces = near * columns
    peers = far * pieces
    owners = peers * cores
    width = -(-pixel_count // (pieces * LANES)) * LANES
    padded = pieces * width
    place = lax.axis_index(group)
    total = held * owners
    params = pltpu.CompilerParams(vmem_limit_bytes=min(60 << 20, (8 << 20) + total * (88 << 10)))

    steps = [0] + sorted(range(1, pieces), key=exchange_order)
    where = jnp.stack([place, lax.axis_index("core")])
    scalars = pl.BlockSpec(memory_space=pltpu.SMEM)
    vectors = pl.BlockSpec(memory_space=pltpu.VMEM)
    distant = (
        projections.reshape(held, 2 * pixel_count),
        particles,
        ctf,
        defocus_group[None, :],
        offsets.T,
        routes.T,
    )
    split = jax.ShapeDtypeStruct((peers, 2 * held, width), bf16)
    piece = jax.ShapeDtypeStruct((2 * rows, width + LANES), bf16)
    in_place = pl.BlockSpec(memory_space=pltpu.HBM)
    refs, *parts = pl.pallas_call(
        functools.partial(prepare_kernel, pixel_count, width, steps, group),
        out_shape=[split] + [piece] * pieces,
        in_specs=[in_place] * len(distant),
        out_specs=[in_place] * (1 + pieces),
        scratch_shapes=[pltpu.VMEM(array.shape, array.dtype) for array in distant]
        + [
            pltpu.VMEM(split.shape, bf16),
            pltpu.VMEM((pieces, 2 * rows, width + LANES), bf16),
            pltpu.VMEM((rows, pixel_count), f32),
            pltpu.VMEM((-(-(3 + route_count) // 8) * 8, -(-rows // LANES) * LANES), f32),
            pltpu.SemaphoreType.DMA((len(distant),)),
            pltpu.SemaphoreType.DMA((1 + pieces,)),
        ],
        compiler_params=pltpu.CompilerParams(vmem_limit_bytes=60 << 20),
        name="prepare",
    )(*distant)
    refs = lax.all_to_all(refs, same_core, split_axis=0, concat_axis=0, tiled=True)
    blocks = [refs] + [lax.ppermute(refs, "core", routes_of(step, cores)) for step in range(1, cores)]
    blocks = [block.transpose(1, 0, 2) for block in blocks]
    parts = list(parts)
    for at in range(1, pieces):
        parts[at] = lax.ppermute(parts[at], group, routes_of(steps[at], pieces))

    column = place * width + jnp.arange(width, dtype=jnp.int32)
    across, down = column // KY, column % KY - KY // 2
    angles = jnp.stack([across, down]).astype(f32) * (2.0 * math.pi / BOX)
    phases = jnp.stack([jnp.cos(angles), jnp.sin(angles)], axis=1).reshape(4, width)
    ctf_here = lax.dynamic_slice_in_dim(
        jnp.pad(ctf, ((0, 0), (0, padded - pixel_count))), place * width, width, 1
    )

    count = pieces * rows
    listings = route_count * SHIFTS * held * columns
    folds = 4 if count % 32 == 0 else 1
    turned, energies = zip(
        *(
            pl.pallas_call(
                turn_kernel,
                out_shape=(
                    jax.ShapeDtypeStruct((2, SHIFTS * held * peers, width), bf16),
                    jax.ShapeDtypeStruct((ctf.shape[0], SHIFTS * held * peers), f32),
                ),
                scratch_shapes=[pltpu.VMEM((held * peers, width), f32)],
                compiler_params=params,
            )(block, ctf_here, phases)
            for block in blocks
        )
    )
    scores, aligned = pl.pallas_call(
        functools.partial(score_kernel, rows, route_count, columns, held, cores, steps),
        out_shape=(
            jax.ShapeDtypeStruct((pieces, count // folds, folds * listings), f32),
            jax.ShapeDtypeStruct((pieces, 2 * rows, width + LANES), bf16),
        ),
        in_specs=[vectors] * (pieces + 2 * cores) + [scalars],
        scratch_shapes=[
            pltpu.VMEM((count, SHIFTS * total), f32),
            pltpu.VMEM((count, LANES), f32),
            pltpu.VMEM((count // folds, folds * listings), f32),
        ],
        compiler_params=params,
        name="score",
    )(*parts, *turned, *energies, where)
    aligned = aligned.reshape(pieces * 2 * rows, width + LANES)

    scores = lax.all_to_all(scores, group, split_axis=0, concat_axis=0, tiled=True)

    kinds = [f32] + [bf16] * (cores - 1)
    *sums, evidence = pl.pallas_call(
        functools.partial(sums_kernel, rows, route_count, columns),
        out_shape=(
            *(jax.ShapeDtypeStruct((2 * held, peers, width), kind) for kind in kinds),
            jax.ShapeDtypeStruct((2 * pieces * rows, LANES), f32),
        ),
        in_specs=[vectors] * 3 + [scalars],
        scratch_shapes=[pltpu.VMEM((count, listings), f32), pltpu.VMEM((2 * count, listings), f32)],
        compiler_params=params,
        name="sums",
    )(scores, aligned, phases, where)
    log_evidence = lax.dynamic_slice_in_dim(evidence, place * 2 * rows, rows, 0)[:, 0]

    merged = sums[0]
    for step in range(1, cores):
        merged = merged + lax.ppermute(sums[step], "core", routes_of(step, cores)).astype(f32)
    merged = merged.astype(bf16).transpose(1, 0, 2)
    merged = lax.all_to_all(merged, same_core, split_axis=0, concat_axis=0, tiled=True)
    data_sum = jnp.sum(merged.reshape(far, pieces, 2 * held, width).astype(f32), axis=0)
    data_sum = data_sum.astype(bf16).reshape(pieces, 2, held, width).transpose(2, 1, 0, 3)
    data_sum = data_sum.reshape(held, 2, padded)[:, :, :pixel_count]
    return (log_evidence, data_sum.reshape(projections.shape))


def solution(mesh):
    groups, orient, columns = (mesh.shape[name] for name in ("groups", "orient", "cls"))
    cores = 2 if orient % 2 == 0 else 1
    near = 2 if orient % (2 * cores) == 0 else 1
    axes = ("groups", "far", "near", "core", "cls")
    along = ("far", "near", "core")
    inner = Mesh(
        mesh.devices.reshape(groups, orient // (near * cores), near, cores, columns), axes
    )
    placed = (
        P(axes, None),
        P("cls", along, None),
        P(),
        P(axes),
        P(axes, None),
        P(axes, None),
    )
    return jax.shard_map(
        expectation,
        mesh=inner,
        in_specs=placed,
        out_specs=(P(axes), P(("groups", "cls"), along, None)),
        check_vma=False,
    )
```

```python
import functools
import math

import jax
import jax.numpy as jnp
from jax import lax
from jax.experimental import pallas as pl
from jax.experimental.pallas import tpu as pltpu
from jax.sharding import Mesh
from jax.sharding import PartitionSpec as P


KX = 86
KY = 192
BOX = 256
LANES = 128
SHIFTS = 5

highest = lax.Precision.HIGHEST
f32 = jnp.float32
bf16 = jnp.bfloat16


def unit_circle(turns):
    quarter = BOX // 4
    quadrant = jnp.floor(turns * (1.0 / quarter) + 0.5)
    angle = (turns - quadrant * quarter) * (2.0 * math.pi / BOX)
    quadrant = quadrant - 4.0 * jnp.floor(quadrant * 0.25)
    square = angle * angle
    sine = angle * (
        1.0
        + square
        * (-1.0 / 6 + square * (1.0 / 120 + square * (-1.0 / 5040 + square * (1.0 / 362880))))
    )
    cosine = 1.0 + square * (
        -0.5 + square * (1.0 / 24 + square * (-1.0 / 720 + square * (1.0 / 40320)))
    )
    odd = (quadrant == 1.0) | (quadrant == 3.0)
    first = jnp.where(odd, sine, cosine)
    second = jnp.where(odd, cosine, sine)
    first = jnp.where((quadrant == 1.0) | (quadrant == 2.0), -first, first)
    second = jnp.where(quadrant >= 2.0, -second, second)
    return first, second


def other(place, step, size):
    if size & (size - 1) == 0:
        return place ^ step
    return lax.rem(place + step, size)


def source(place, step, size):
    if size & (size - 1) == 0:
        return place ^ step
    return lax.rem(place + size - step, size)


def exchange_order(step):
    return (step.bit_count() == 2, -step.bit_count(), step)


def routes_of(step, size):
    return [(i, int(other(i, step, size))) for i in range(size)]


def split_refs(pixel_count, width, refs, out):
    held = refs.shape[0]
    pieces = -(-pixel_count // width)
    for piece in range(pieces):
        low = piece * width
        size = min(width, pixel_count - low)
        for half in range(2):
            values = refs[:, half * pixel_count + low : half * pixel_count + low + size]
            for copy in range(piece, out.shape[0], pieces):
                out[copy, half * held : (half + 1) * held, 0:size] = values
                if size < width:
                    out[copy, half * held : (half + 1) * held, size:width] = jnp.zeros(
                        (held, width - size), bf16
                    )


def prepare_kernel(pixel_count, width, steps, group, *refs):
    distant, (split, *outs), rest = refs[:6], refs[6 : 7 + len(steps)], refs[7 + len(steps) :]
    near, (split_here, whole, ctf_rows, table, arrived, left) = rest[:6], rest[6:]
    copies = [
        pltpu.make_async_copy(far, here, arrived.at[i])
        for i, (far, here) in enumerate(zip(distant, near))
    ]
    for copy in copies:
        copy.start()
    copies[0].wait()
    split_refs(pixel_count, width, near[0], split_here)
    sent = [pltpu.make_async_copy(split_here, split, left.at[0])]
    sent[0].start()
    for copy in copies[2:]:
        copy.wait()
    align(pixel_count, width, *near[1:], whole, ctf_rows, table, copies[1])
    place = lax.axis_index(group)
    for step, out in zip(steps, outs):
        piece = whole.at[other(place, step, len(steps))]
        sent.append(pltpu.make_async_copy(piece, out, left.at[len(sent)]))
        sent[-1].start()
    for copy in sent:
        copy.wait()


def align(
    pixel_count, width, images, ctf, groups, offsets, routes, whole, ctf_rows, table, coming
):
    rows = images.shape[0]
    pieces = whole.shape[0]
    route_count = routes.shape[0]
    table[...] = jnp.zeros(table.shape, f32)
    table[0:2, 0:rows] = offsets[...].astype(f32)
    table[2:3, 0:rows] = groups[...].astype(f32)
    table[3 : 3 + route_count, 0:rows] = routes[...].astype(f32)
    facts = table[...].T[0:rows]
    shift_across, shift_down, group = facts[:, 0:1], facts[:, 1:2], facts[:, 2:3]
    block = math.lcm(LANES, KY)
    per_block = block // LANES
    onehot = (
        group == lax.broadcasted_iota(jnp.int32, (rows, ctf.shape[0]), 1).astype(f32)
    ).astype(bf16)
    ctf_rows[...] = jnp.dot(onehot, ctf[...], preferred_element_type=f32)
    lane = lax.broadcasted_iota(jnp.int32, (rows, block), 1)
    across = jnp.zeros((rows, block), jnp.int32)
    for step in range(1, block // KY):
        across = across + (lane >= step * KY).astype(jnp.int32)
    down = lane - across * KY - KY // 2
    base_cos, base_sin = unit_circle(
        across.astype(f32) * shift_across + down.astype(f32) * shift_down
    )
    blocks = -(-pixel_count // block)
    start = lax.broadcasted_iota(jnp.int32, (rows, blocks), 1) * (block // KY)
    start_cos, start_sin = unit_circle(start.astype(f32) * shift_across)
    coming.wait()
    for piece in range(pieces):
        for part in range(width // LANES):
            low = piece * width + part * LANES
            here = slice(part * LANES, (part + 1) * LANES)
            if low >= pixel_count:
                whole[piece, :, here] = jnp.zeros((2 * rows, LANES), bf16)
                continue
            turn, step = divmod(low // LANES, per_block)
            bc = base_cos[:, step * LANES : (step + 1) * LANES]
            bs = base_sin[:, step * LANES : (step + 1) * LANES]
            rc = start_cos[:, turn : turn + 1]
            rs = start_sin[:, turn : turn + 1]
            cosine = bc * rc - bs * rs
            sine = bs * rc + bc * rs
            scale = ctf_rows[:, low : low + LANES]
            real = images[:, low : low + LANES].astype(f32)
            imag = images[:, pixel_count + low : pixel_count + low + LANES].astype(f32)
            first = (real * cosine + imag * sine) * scale
            second = (imag * cosine - real * sine) * scale
            whole[piece, :, here] = jnp.concatenate([first, second], axis=0).astype(bf16)
    lane = lax.broadcasted_iota(jnp.int32, (rows, LANES), 1)
    notes = jnp.where(lane == route_count, group, 0.0)
    for r in range(route_count):
        notes = jnp.where(lane == r, facts[:, 3 + r : 4 + r], notes)
    notes = jnp.concatenate([notes, notes], axis=0).astype(bf16)
    for piece in range(pieces):
        whole[piece, :, width : width + LANES] = notes


def spot_table(spot, spots):
    row = lax.broadcasted_iota(jnp.int32, (spots, spot.shape[1]), 0).astype(f32)
    return jnp.where(row == spot, 1.0, 0.0).astype(bf16)


def block_facts(held, peers, blocks, columns, core_here):
    each = SHIFTS * held * peers
    lane = lax.broadcasted_iota(jnp.int32, (1, each * blocks), 1)
    inside, peer = lax.rem(lane, each), lax.rem(lane, peers)
    core = source(core_here, lane // each, blocks)
    direction = (peer // columns) * blocks + core
    spot = (inside // peers) * columns + lax.rem(peer, columns)
    return direction.astype(f32), spot.astype(f32)


def turn_kernel(refs, ctf, phases, turned, energy, power):
    width = phases.shape[1]
    held = refs.shape[0] // 2
    total = held * refs.shape[1]
    for low in range(0, width, LANES):
        here = slice(low, low + LANES)
        real = jnp.concatenate([refs[k, :, here] for k in range(held)], axis=0)
        imag = jnp.concatenate([refs[held + k, :, here] for k in range(held)], axis=0)
        turned[0, 0:total, here] = real
        turned[1, 0:total, here] = imag
        real, imag = real.astype(f32), imag.astype(f32)
        power[:, here] = real * real + imag * imag
        for axis in range(2):
            cosine = phases[2 * axis : 2 * axis + 1, here]
            sine = phases[2 * axis + 1 : 2 * axis + 2, here]
            rc, rs, ic, is_ = real * cosine, real * sine, imag * cosine, imag * sine
            at = (1 + 2 * axis) * total
            turned[0, at : at + total, here] = (rc - is_).astype(bf16)
            turned[1, at : at + total, here] = (rs + ic).astype(bf16)
            at = at + total
            turned[0, at : at + total, here] = (rc + is_).astype(bf16)
            turned[1, at : at + total, here] = (ic - rs).astype(bf16)
    table = ctf[...].astype(f32)
    half = 0.5 * lax.dot_general(
        table * table,
        power[...],
        (((1,), (1,)), ((), ())),
        precision=highest,
        preferred_element_type=f32,
    )
    energy[...] = jnp.concatenate([half] * SHIFTS, axis=1)


def score_kernel(rows, route_count, columns, held, cores, steps, *refs_all):
    count = len(steps)
    parts, blocks, energies = refs_all[:count], refs_all[count:][:cores], refs_all[count + cores :][:cores]
    out, aligned, dense, notes, packed = refs_all[count + 2 * cores :]
    place, core = lax.axis_index(("near", "cls")), lax.axis_index("core")
    width = blocks[0].shape[2]
    each = blocks[0].shape[1]
    for step, part in zip(steps, parts):
        aligned[source(place, step, count)] = part[...]
    across = (((1,), (1,)), ((), ()))
    images = aligned[:, :, 0:width].reshape(2 * rows * count, width)
    for block, turned in enumerate(blocks):
        real = lax.dot_general(images, turned[0], across, preferred_element_type=f32)
        imag = lax.dot_general(images, turned[1], across, preferred_element_type=f32)
        for at in range(count):
            low = 2 * rows * at
            dense[at * rows : (at + 1) * rows, block * each : (block + 1) * each] = (
                real[low : low + rows, :] + imag[low + rows : low + 2 * rows, :]
            )
    for at in range(count):
        mine = slice(at * rows, (at + 1) * rows)
        notes[mine, :] = aligned[at, 0:rows, width : width + LANES].astype(f32)
    energy = jnp.concatenate([energy[...] for energy in energies], axis=1)
    facts = notes[...]
    values = dense[...]
    for g in range(energy.shape[0]):
        values = values - jnp.where(
            facts[:, route_count : route_count + 1] == float(g), energy[g : g + 1, :], 0.0
        )
    first = values.astype(bf16)
    rest = values - first.astype(f32)
    second = rest.astype(bf16)
    third = (rest - second.astype(f32)).astype(bf16)
    terms = [first.astype(f32), second.astype(f32), third.astype(f32)]
    direction, spot = block_facts(held, each // (SHIFTS * held), cores, columns, core)
    spots = SHIFTS * held * columns
    particles = rows * count
    stacked = []
    for r in range(route_count):
        listed = facts[:, r : r + 1] == direction
        stacked += [jnp.where(listed, term, 0.0).astype(bf16) for term in terms]
    chosen = lax.dot_general(
        jnp.concatenate(stacked, axis=0),
        spot_table(spot, spots),
        across,
        preferred_element_type=f32,
    )
    height = out.shape[1]
    for r in range(route_count):
        low = r * len(terms) * particles
        mine = chosen[low : low + particles]
        for term in range(1, len(terms)):
            mine = mine + chosen[low + term * particles : low + (term + 1) * particles]
        for block in range(particles // height):
            at = (block * route_count + r) * spots
            packed[:, at : at + spots] = mine[block * height : (block + 1) * height]
    for copy in range(out.shape[0]):
        out[copy] = packed[...]


def turn_back(weights_real, weights_imag, aligned, phases, out):
    width = phases.shape[1]
    held, peers = out.shape[0] // 2, out.shape[1]
    total = held * peers
    chunk = 2 * LANES
    for low in range(0, width, chunk):
        high = min(low + chunk, width)
        images = aligned[:, low:high]
        real = jnp.dot(weights_real, images, preferred_element_type=f32)
        imag = jnp.dot(weights_imag, images, preferred_element_type=f32)
        u = [real[t * total : (t + 1) * total] for t in range(SHIFTS)]
        v = [imag[t * total : (t + 1) * total] for t in range(SHIFTS)]
        first, second = u[0], v[0]
        for axis in range(2):
            cosine = phases[2 * axis : 2 * axis + 1, low:high]
            sine = phases[2 * axis + 1 : 2 * axis + 2, low:high]
            one, two = 1 + 2 * axis, 2 + 2 * axis
            first = first + (u[one] + u[two]) * cosine + (v[one] - v[two]) * sine
            second = second + (v[one] + v[two]) * cosine - (u[one] - u[two]) * sine
        for k in range(held):
            mine = slice(k * peers, (k + 1) * peers)
            out[k, :, low:high] = first[mine].astype(out.dtype)
            out[held + k, :, low:high] = second[mine].astype(out.dtype)


def weigh_kernel(rows, route_count, columns, held, cores, scores, aligned, phases, *outs_and_scratch):
    core = lax.axis_index("core")
    *outs, own_real, own_imag, evidence, tall, wide = outs_and_scratch
    width = phases.shape[1]
    count = aligned.shape[0]
    each = own_real.shape[0]
    peers = each // (SHIFTS * held)
    height = scores.shape[1]
    blocks = count // (2 * height)
    listings = scores.shape[2] // blocks
    summed = scores[0]
    for part in range(1, scores.shape[0]):
        summed = summed + scores[part]
    for block in range(blocks):
        tall[block * height : (block + 1) * height, :] = summed[
            :, block * listings : (block + 1) * listings
        ]
    for part in range(count // (2 * rows)):
        values = tall[part * rows : (part + 1) * rows, :]
        at = 2 * rows * part
        wide[at : at + rows, :] = values
        wide[at + rows : at + 2 * rows, :] = values
    values = wide[...]
    peak = jnp.max(values, axis=1, keepdims=True)
    mass = jnp.sum(jnp.exp(values - peak), axis=1, keepdims=True)
    log_evidence = peak + jnp.log(mass)
    evidence[...] = jnp.broadcast_to(log_evidence, evidence.shape)
    listed_weights = jnp.exp(values - log_evidence).astype(bf16)
    notes = aligned[:, width : width + LANES].astype(f32)
    direction, spot = block_facts(held, peers, cores, columns, core)
    spots = listings // route_count
    spread = spot_table(spot, spots)
    weights = jnp.zeros((count, each * cores), f32)
    for r in range(route_count):
        placed = jnp.dot(
            listed_weights[:, r * spots : (r + 1) * spots], spread, preferred_element_type=f32
        )
        weights = jnp.where(notes[:, r : r + 1] == direction, placed, weights)
    row = lax.broadcasted_iota(jnp.int32, (count, 1), 0)
    first_half = jnp.zeros((count, 1), jnp.bool_)
    for part in range(count // (2 * rows)):
        at = 2 * rows * part
        first_half = first_half | ((row >= at) & (row < at + rows))
    weights_real = jnp.where(first_half, weights, 0.0).T.astype(bf16)
    weights_imag = jnp.where(first_half, 0.0, weights).T.astype(bf16)
    own_real[...] = weights_real[0:each]
    own_imag[...] = weights_imag[0:each]
    for step, out in enumerate(outs, 1):
        block = slice(step * each, (step + 1) * each)
        turn_back(weights_real[block], weights_imag[block], aligned, phases, out)


def own_kernel(weights_real, weights_imag, aligned, phases, out):
    turn_back(weights_real[...], weights_imag[...], aligned, phases, out)


def expectation(particles, projections, ctf, defocus_group, offsets, routes):
    pixel_count = KX * KY
    rows = particles.shape[0]
    route_count = routes.shape[1]
    held = projections.shape[0] * projections.shape[1]
    far, near, cores, columns = (
        lax.axis_size(name) for name in ("far", "near", "core", "cls")
    )
    group = ("near", "cls")
    same_core = ("far", "near", "cls")
    pieces = near * columns
    peers = far * pieces
    owners = peers * cores
    width = -(-pixel_count // (pieces * LANES)) * LANES
    padded = pieces * width
    place = lax.axis_index(group)
    total = held * owners
    params = pltpu.CompilerParams(vmem_limit_bytes=min(60 << 20, (8 << 20) + total * (88 << 10)))

    steps = [0] + sorted(range(1, pieces), key=exchange_order)
    distant = (
        projections.reshape(held, 2 * pixel_count),
        particles,
        ctf,
        defocus_group[None, :],
        offsets.T,
        routes.T,
    )
    split = jax.ShapeDtypeStruct((peers, 2 * held, width), bf16)
    piece = jax.ShapeDtypeStruct((2 * rows, width + LANES), bf16)
    in_place = pl.BlockSpec(memory_space=pltpu.HBM)
    refs, *parts = pl.pallas_call(
        functools.partial(prepare_kernel, pixel_count, width, steps, group),
        out_shape=[split] + [piece] * pieces,
        in_specs=[in_place] * len(distant),
        out_specs=[in_place] * (1 + pieces),
        scratch_shapes=[pltpu.VMEM(array.shape, array.dtype) for array in distant]
        + [
            pltpu.VMEM(split.shape, bf16),
            pltpu.VMEM((pieces, 2 * rows, width + LANES), bf16),
            pltpu.VMEM((rows, pixel_count), f32),
            pltpu.VMEM((-(-(3 + route_count) // 8) * 8, -(-rows // LANES) * LANES), f32),
            pltpu.SemaphoreType.DMA((len(distant),)),
            pltpu.SemaphoreType.DMA((1 + pieces,)),
        ],
        compiler_params=pltpu.CompilerParams(vmem_limit_bytes=60 << 20),
        name="prepare",
    )(*distant)
    refs = lax.all_to_all(refs, same_core, split_axis=0, concat_axis=0, tiled=True)
    blocks = [refs] + [lax.ppermute(refs, "core", routes_of(step, cores)) for step in range(1, cores)]
    blocks = [block.transpose(1, 0, 2) for block in blocks]
    parts = list(parts)
    for at in range(1, pieces):
        parts[at] = lax.ppermute(parts[at], group, routes_of(steps[at], pieces))

    column = place * width + jnp.arange(width, dtype=jnp.int32)
    across, down = column // KY, column % KY - KY // 2
    angles = jnp.stack([across, down]).astype(f32) * (2.0 * math.pi / BOX)
    phases = jnp.stack([jnp.cos(angles), jnp.sin(angles)], axis=1).reshape(4, width)
    ctf_here = lax.dynamic_slice_in_dim(
        jnp.pad(ctf, ((0, 0), (0, padded - pixel_count))), place * width, width, 1
    )

    count = pieces * rows
    listings = route_count * SHIFTS * held * columns
    folds = 4 if count % 32 == 0 else 1
    turned, energies = zip(
        *(
            pl.pallas_call(
                turn_kernel,
                out_shape=(
                    jax.ShapeDtypeStruct((2, SHIFTS * held * peers, width), bf16),
                    jax.ShapeDtypeStruct((ctf.shape[0], SHIFTS * held * peers), f32),
                ),
                scratch_shapes=[pltpu.VMEM((held * peers, width), f32)],
                compiler_params=params,
            )(block, ctf_here, phases)
            for block in blocks
        )
    )
    scores, aligned = pl.pallas_call(
        functools.partial(score_kernel, rows, route_count, columns, held, cores, steps),
        out_shape=(
            jax.ShapeDtypeStruct((pieces, count // folds, folds * listings), f32),
            jax.ShapeDtypeStruct((pieces, 2 * rows, width + LANES), bf16),
        ),
        scratch_shapes=[
            pltpu.VMEM((count, SHIFTS * total), f32),
            pltpu.VMEM((count, LANES), f32),
            pltpu.VMEM((count // folds, folds * listings), f32),
        ],
        compiler_params=params,
        name="score",
    )(*parts, *turned, *energies)
    aligned = aligned.reshape(pieces * 2 * rows, width + LANES)

    scores = lax.all_to_all(scores, group, split_axis=0, concat_axis=0, tiled=True)

    each = SHIFTS * held * peers
    block = (2 * held, peers, width)
    *sums, own_real, own_imag, evidence = pl.pallas_call(
        functools.partial(weigh_kernel, rows, route_count, columns, held, cores),
        out_shape=(
            *[jax.ShapeDtypeStruct(block, bf16)] * (cores - 1),
            *[jax.ShapeDtypeStruct((each, 2 * count), bf16)] * 2,
            jax.ShapeDtypeStruct((2 * count, LANES), f32),
        ),
        scratch_shapes=[pltpu.VMEM((count, listings), f32), pltpu.VMEM((2 * count, listings), f32)],
        compiler_params=params,
        name="weigh",
    )(scores, aligned, phases)
    sums = [
        lax.ppermute(array, "core", routes_of(step, cores))
        for step, array in enumerate(sums, 1)
    ]
    merged = pl.pallas_call(
        own_kernel,
        out_shape=jax.ShapeDtypeStruct(block, f32),
        compiler_params=params,
        cost_estimate=pl.CostEstimate(
            flops=8 * each * count * width, bytes_accessed=4 << 20, transcendentals=0
        ),
        name="own",
    )(own_real, own_imag, aligned, phases)
    log_evidence = lax.dynamic_slice_in_dim(evidence, place * 2 * rows, rows, 0)[:, 0]

    for array in sums:
        merged = merged + array.astype(f32)
    merged = merged.astype(bf16).transpose(1, 0, 2)
    merged = lax.all_to_all(merged, same_core, split_axis=0, concat_axis=0, tiled=True)
    data_sum = jnp.sum(merged.reshape(far, pieces, 2 * held, width).astype(f32), axis=0)
    data_sum = data_sum.astype(bf16).reshape(pieces, 2, held, width).transpose(2, 1, 0, 3)
    data_sum = data_sum.reshape(held, 2, padded)[:, :, :pixel_count]
    return (log_evidence, data_sum.reshape(projections.shape))


def solution(mesh):
    groups, orient, columns = (mesh.shape[name] for name in ("groups", "orient", "cls"))
    cores = 2 if orient % 2 == 0 else 1
    near = 2 if orient % (2 * cores) == 0 else 1
    axes = ("groups", "far", "near", "core", "cls")
    along = ("far", "near", "core")
    inner = Mesh(
        mesh.devices.reshape(groups, orient // (near * cores), near, cores, columns), axes
    )
    placed = (
        P(axes, None),
        P("cls", along, None),
        P(),
        P(axes),
        P(axes, None),
        P(axes, None),
    )
    return jax.shard_map(
        expectation,
        mesh=inner,
        in_specs=placed,
        out_specs=(P(axes), P(("groups", "cls"), along, None)),
        check_vma=False,
    )
```

```python
import functools
import math

import jax
import jax.numpy as jnp
from jax import lax
from jax.experimental import pallas as pl
from jax.experimental.pallas import tpu as pltpu
from jax.sharding import Mesh
from jax.sharding import PartitionSpec as P


KX = 86
KY = 192
BOX = 256
LANES = 128
SHIFTS = 5

highest = lax.Precision.HIGHEST
f32 = jnp.float32
bf16 = jnp.bfloat16


def unit_circle(turns):
    quarter = BOX // 4
    quadrant = jnp.floor(turns * (1.0 / quarter) + 0.5)
    angle = (turns - quadrant * quarter) * (2.0 * math.pi / BOX)
    quadrant = quadrant - 4.0 * jnp.floor(quadrant * 0.25)
    square = angle * angle
    sine = angle * (
        1.0
        + square
        * (-1.0 / 6 + square * (1.0 / 120 + square * (-1.0 / 5040 + square * (1.0 / 362880))))
    )
    cosine = 1.0 + square * (
        -0.5 + square * (1.0 / 24 + square * (-1.0 / 720 + square * (1.0 / 40320)))
    )
    odd = (quadrant == 1.0) | (quadrant == 3.0)
    first = jnp.where(odd, sine, cosine)
    second = jnp.where(odd, cosine, sine)
    first = jnp.where((quadrant == 1.0) | (quadrant == 2.0), -first, first)
    second = jnp.where(quadrant >= 2.0, -second, second)
    return first, second


def other(place, step, size):
    if size & (size - 1) == 0:
        return place ^ step
    return lax.rem(place + step, size)


def source(place, step, size):
    if size & (size - 1) == 0:
        return place ^ step
    return lax.rem(place + size - step, size)


def exchange_order(step):
    return (step.bit_count() == 2, -step.bit_count(), step)


def routes_of(step, size):
    return [(i, int(other(i, step, size))) for i in range(size)]


def layout(pixel_count, pieces, facts):
    main = pixel_count // (pieces * LANES) * LANES
    share = -(-(pixel_count - pieces * main) // pieces)
    width = main + LANES * (1 if share + facts <= LANES else 2)
    return main, share, width, share if width == main + LANES else 0


def split_refs(pixel_count, main, share, refs, out):
    held, width = refs.shape[0], out.shape[2]
    pieces = pixel_count // main if share == 0 else (pixel_count - 1) // (main + share) + 1
    for half in range(2):
        start = half * pixel_count
        left = refs[:, start + pieces * main : start + pixel_count].astype(f32)
        for piece in range(pieces):
            tail = left[:, piece * share : (piece + 1) * share]
            empty = jnp.zeros((held, width - main - tail.shape[1]), f32)
            tail = jnp.concatenate([tail, empty], axis=1).astype(bf16)
            values = refs[:, start + piece * main : start + (piece + 1) * main]
            for copy in range(piece, out.shape[0], pieces):
                out[copy, half * held : (half + 1) * held, 0:main] = values
                out[copy, half * held : (half + 1) * held, main:width] = tail


def own_ctf(pixel_count, plan, pieces, place, ctf, out):
    main, share, width, _ = plan
    for low in range(0, main, LANES):
        start = pl.multiple_of(place * main + low, LANES)
        out[:, low : low + LANES] = ctf[:, pl.ds(start, LANES)]
    left = ctf[:, pieces * main : pixel_count].astype(f32)
    tail = jnp.zeros((ctf.shape[0], width - main), f32)
    for piece in range(pieces):
        mine = left[:, piece * share : (piece + 1) * share]
        empty = jnp.zeros((ctf.shape[0], width - main - mine.shape[1]), f32)
        tail = jnp.where(place == piece, jnp.concatenate([mine, empty], axis=1), tail)
    out[:, main:width] = tail.astype(bf16)


def prepare_kernel(pixel_count, plan, steps, group, *refs):
    distant, (split, ctf_out, *outs), rest = refs[:6], refs[6 : 8 + len(steps)], refs[8 + len(steps) :]
    near, (split_here, ctf_here, whole, ctf_rows, table, arrived, left) = rest[:6], rest[6:]
    copies = [
        pltpu.make_async_copy(far, here, arrived.at[i])
        for i, (far, here) in enumerate(zip(distant, near))
    ]
    for copy in copies:
        copy.start()
    copies[0].wait()
    split_refs(pixel_count, *plan[:2], near[0], split_here)
    sent = [pltpu.make_async_copy(split_here, split, left.at[0])]
    sent[0].start()
    for copy in copies[2:]:
        copy.wait()
    place = lax.axis_index(group)
    own_ctf(pixel_count, plan, len(steps), place, near[2], ctf_here)
    sent.append(pltpu.make_async_copy(ctf_here, ctf_out, left.at[1]))
    sent[1].start()
    align(pixel_count, plan, *near[1:], whole, ctf_rows, table, copies[1])
    for step, out in zip(steps, outs):
        piece = whole.at[other(place, step, len(steps))]
        sent.append(pltpu.make_async_copy(piece, out, left.at[len(sent)]))
        sent[-1].start()
    for copy in sent:
        copy.wait()


def align(
    pixel_count, plan, images, ctf, groups, offsets, routes, whole, ctf_rows, table, coming
):
    rows = images.shape[0]
    pieces = whole.shape[0]
    route_count = routes.shape[0]
    table[...] = jnp.zeros(table.shape, f32)
    table[0:2, 0:rows] = offsets[...].astype(f32)
    table[2:3, 0:rows] = groups[...].astype(f32)
    table[3 : 3 + route_count, 0:rows] = routes[...].astype(f32)
    facts = table[...].T[0:rows]
    shift_across, shift_down, group = facts[:, 0:1], facts[:, 1:2], facts[:, 2:3]
    block = math.lcm(LANES, KY)
    per_block = block // LANES
    onehot = (
        group == lax.broadcasted_iota(jnp.int32, (rows, ctf.shape[0]), 1).astype(f32)
    ).astype(bf16)
    ctf_rows[...] = jnp.dot(onehot, ctf[...], preferred_element_type=f32)
    lane = lax.broadcasted_iota(jnp.int32, (rows, block), 1)
    across = jnp.zeros((rows, block), jnp.int32)
    for step in range(1, block // KY):
        across = across + (lane >= step * KY).astype(jnp.int32)
    down = lane - across * KY - KY // 2
    base_cos, base_sin = unit_circle(
        across.astype(f32) * shift_across + down.astype(f32) * shift_down
    )
    blocks = -(-pixel_count // block)
    start = lax.broadcasted_iota(jnp.int32, (rows, blocks), 1) * (block // KY)
    start_cos, start_sin = unit_circle(start.astype(f32) * shift_across)
    coming.wait()

    def tile(low):
        turn, step = divmod(low // LANES, per_block)
        bc = base_cos[:, step * LANES : (step + 1) * LANES]
        bs = base_sin[:, step * LANES : (step + 1) * LANES]
        rc = start_cos[:, turn : turn + 1]
        rs = start_sin[:, turn : turn + 1]
        cosine = bc * rc - bs * rs
        sine = bs * rc + bc * rs
        scale = ctf_rows[:, low : low + LANES]
        real = images[:, low : low + LANES].astype(f32)
        imag = images[:, pixel_count + low : pixel_count + low + LANES].astype(f32)
        first = (real * cosine + imag * sine) * scale
        second = (imag * cosine - real * sine) * scale
        return jnp.concatenate([first, second], axis=0)

    main, share, width, spare = plan
    for piece in range(pieces):
        for low in range(0, main, LANES):
            whole[piece, :, low : low + LANES] = tile(piece * main + low).astype(bf16)
    left = [tile(low) for low in range(pieces * main, pixel_count, LANES)]
    lane = lax.broadcasted_iota(jnp.int32, (rows, LANES), 1)
    notes = jnp.where(lane == spare + route_count, group, 0.0)
    for r in range(route_count):
        notes = jnp.where(lane == spare + r, facts[:, 3 + r : 4 + r], notes)
    notes = jnp.concatenate([notes, notes], axis=0)
    left = jnp.concatenate(left, axis=1) if left else notes[:, 0:0]
    for piece in range(pieces):
        mine = left[:, piece * share : (piece + 1) * share]
        if width > main + LANES:
            empty = jnp.zeros((2 * rows, width - LANES - main - mine.shape[1]), f32)
            tail = jnp.concatenate([mine, empty, notes], axis=1)
        else:
            tail = jnp.concatenate([mine, notes[:, mine.shape[1] :]], axis=1)
        whole[piece, :, main:width] = tail.astype(bf16)


def spot_table(spot, spots):
    row = lax.broadcasted_iota(jnp.int32, (spots, spot.shape[1]), 0).astype(f32)
    return jnp.where(row == spot, 1.0, 0.0).astype(bf16)


def block_facts(held, peers, blocks, columns, core_here):
    each = SHIFTS * held * peers
    lane = lax.broadcasted_iota(jnp.int32, (1, each * blocks), 1)
    inside, peer = lax.rem(lane, each), lax.rem(lane, peers)
    core = source(core_here, lane // each, blocks)
    direction = (peer // columns) * blocks + core
    spot = (inside // peers) * columns + lax.rem(peer, columns)
    return direction.astype(f32), spot.astype(f32)


def turn_kernel(refs, ctf, phases, turned, energy, power):
    width = phases.shape[1]
    held = refs.shape[0] // 2
    total = held * refs.shape[1]
    for low in range(0, width, LANES):
        here = slice(low, low + LANES)
        real = jnp.concatenate([refs[k, :, here] for k in range(held)], axis=0)
        imag = jnp.concatenate([refs[held + k, :, here] for k in range(held)], axis=0)
        turned[0, 0:total, here] = real
        turned[1, 0:total, here] = imag
        real, imag = real.astype(f32), imag.astype(f32)
        power[:, here] = real * real + imag * imag
        for axis in range(2):
            cosine = phases[2 * axis : 2 * axis + 1, here]
            sine = phases[2 * axis + 1 : 2 * axis + 2, here]
            rc, rs, ic, is_ = real * cosine, real * sine, imag * cosine, imag * sine
            at = (1 + 2 * axis) * total
            turned[0, at : at + total, here] = (rc - is_).astype(bf16)
            turned[1, at : at + total, here] = (rs + ic).astype(bf16)
            at = at + total
            turned[0, at : at + total, here] = (rc + is_).astype(bf16)
            turned[1, at : at + total, here] = (ic - rs).astype(bf16)
    table = ctf[...].astype(f32)
    half = 0.5 * lax.dot_general(
        table * table,
        power[...],
        (((1,), (1,)), ((), ())),
        precision=highest,
        preferred_element_type=f32,
    )
    energy[...] = jnp.concatenate([half] * SHIFTS, axis=1)


def score_kernel(rows, route_count, columns, held, cores, steps, spare, *refs_all):
    count = len(steps)
    parts, blocks, energies = refs_all[:count], refs_all[count:][:cores], refs_all[count + cores :][:cores]
    out, aligned, dense, notes, packed = refs_all[count + 2 * cores :]
    place, core = lax.axis_index(("near", "cls")), lax.axis_index("core")
    width = blocks[0].shape[2]
    each = blocks[0].shape[1]
    for step, part in zip(steps, parts):
        aligned[source(place, step, count)] = part[...]
    across = (((1,), (1,)), ((), ()))
    images = aligned[:, :, 0:width].reshape(2 * rows * count, width)
    for block, turned in enumerate(blocks):
        real = lax.dot_general(images, turned[0], across, preferred_element_type=f32)
        imag = lax.dot_general(images, turned[1], across, preferred_element_type=f32)
        for at in range(count):
            low = 2 * rows * at
            dense[at * rows : (at + 1) * rows, block * each : (block + 1) * each] = (
                real[low : low + rows, :] + imag[low + rows : low + 2 * rows, :]
            )
    for at in range(count):
        mine = slice(at * rows, (at + 1) * rows)
        notes[mine, :] = aligned[at, 0:rows, width - LANES : width].astype(f32)
    energy = jnp.concatenate([energy[...] for energy in energies], axis=1)
    facts = notes[...]
    values = dense[...]
    for g in range(energy.shape[0]):
        values = values - jnp.where(
            facts[:, spare + route_count : spare + route_count + 1] == float(g), energy[g : g + 1, :], 0.0
        )
    first = values.astype(bf16)
    rest = values - first.astype(f32)
    second = rest.astype(bf16)
    third = (rest - second.astype(f32)).astype(bf16)
    terms = [first.astype(f32), second.astype(f32), third.astype(f32)]
    direction, spot = block_facts(held, each // (SHIFTS * held), cores, columns, core)
    spots = SHIFTS * held * columns
    particles = rows * count
    stacked = []
    for r in range(route_count):
        listed = facts[:, spare + r : spare + r + 1] == direction
        stacked += [jnp.where(listed, term, 0.0).astype(bf16) for term in terms]
    chosen = lax.dot_general(
        jnp.concatenate(stacked, axis=0),
        spot_table(spot, spots),
        across,
        preferred_element_type=f32,
    )
    height = out.shape[1]
    for r in range(route_count):
        low = r * len(terms) * particles
        mine = chosen[low : low + particles]
        for term in range(1, len(terms)):
            mine = mine + chosen[low + term * particles : low + (term + 1) * particles]
        for block in range(particles // height):
            at = (block * route_count + r) * spots
            packed[:, at : at + spots] = mine[block * height : (block + 1) * height]
    for copy in range(out.shape[0]):
        out[copy] = packed[...]


def turn_back(weights_real, weights_imag, aligned, phases, out):
    width = phases.shape[1]
    held, peers = out.shape[0] // 2, out.shape[1]
    total = held * peers
    chunk = 2 * LANES
    for low in range(0, width, chunk):
        high = min(low + chunk, width)
        images = aligned[:, low:high]
        real = jnp.dot(weights_real, images, preferred_element_type=f32)
        imag = jnp.dot(weights_imag, images, preferred_element_type=f32)
        u = [real[t * total : (t + 1) * total] for t in range(SHIFTS)]
        v = [imag[t * total : (t + 1) * total] for t in range(SHIFTS)]
        first, second = u[0], v[0]
        for axis in range(2):
            cosine = phases[2 * axis : 2 * axis + 1, low:high]
            sine = phases[2 * axis + 1 : 2 * axis + 2, low:high]
            one, two = 1 + 2 * axis, 2 + 2 * axis
            first = first + (u[one] + u[two]) * cosine + (v[one] - v[two]) * sine
            second = second + (v[one] + v[two]) * cosine - (u[one] - u[two]) * sine
        for k in range(held):
            mine = slice(k * peers, (k + 1) * peers)
            out[k, :, low:high] = first[mine].astype(out.dtype)
            out[held + k, :, low:high] = second[mine].astype(out.dtype)


def weigh_kernel(rows, route_count, columns, held, cores, spare, scores, aligned, phases, *outs_and_scratch):
    core = lax.axis_index("core")
    *outs, own_real, own_imag, evidence, tall, wide = outs_and_scratch
    width = phases.shape[1]
    count = aligned.shape[0]
    each = own_real.shape[0]
    peers = each // (SHIFTS * held)
    height = scores.shape[1]
    blocks = count // (2 * height)
    listings = scores.shape[2] // blocks
    summed = scores[0]
    for part in range(1, scores.shape[0]):
        summed = summed + scores[part]
    for block in range(blocks):
        tall[block * height : (block + 1) * height, :] = summed[
            :, block * listings : (block + 1) * listings
        ]
    for part in range(count // (2 * rows)):
        values = tall[part * rows : (part + 1) * rows, :]
        at = 2 * rows * part
        wide[at : at + rows, :] = values
        wide[at + rows : at + 2 * rows, :] = values
    values = wide[...]
    peak = jnp.max(values, axis=1, keepdims=True)
    mass = jnp.sum(jnp.exp(values - peak), axis=1, keepdims=True)
    log_evidence = peak + jnp.log(mass)
    evidence[...] = jnp.broadcast_to(log_evidence, evidence.shape)
    listed_weights = jnp.exp(values - log_evidence).astype(bf16)
    notes = aligned[:, width - LANES : width].astype(f32)
    direction, spot = block_facts(held, peers, cores, columns, core)
    spots = listings // route_count
    spread = spot_table(spot, spots)
    weights = jnp.zeros((count, each * cores), f32)
    for r in range(route_count):
        placed = jnp.dot(
            listed_weights[:, r * spots : (r + 1) * spots], spread, preferred_element_type=f32
        )
        weights = jnp.where(notes[:, spare + r : spare + r + 1] == direction, placed, weights)
    row = lax.broadcasted_iota(jnp.int32, (count, 1), 0)
    first_half = jnp.zeros((count, 1), jnp.bool_)
    for part in range(count // (2 * rows)):
        at = 2 * rows * part
        first_half = first_half | ((row >= at) & (row < at + rows))
    weights_real = jnp.where(first_half, weights, 0.0).T.astype(bf16)
    weights_imag = jnp.where(first_half, 0.0, weights).T.astype(bf16)
    own_real[...] = weights_real[0:each]
    own_imag[...] = weights_imag[0:each]
    for step, out in enumerate(outs, 1):
        block = slice(step * each, (step + 1) * each)
        turn_back(weights_real[block], weights_imag[block], aligned, phases, out)


def own_kernel(weights_real, weights_imag, aligned, phases, out):
    turn_back(weights_real[...], weights_imag[...], aligned, phases, out)


def collect_kernel(far, main, share, parts, out):
    pieces, held = parts.shape[0] // far, out.shape[0]
    pixel_count = out.shape[1] // 2
    tails = []
    for piece in range(pieces):
        total = parts[piece].astype(f32)
        for part in range(1, far):
            total = total + parts[part * pieces + piece].astype(f32)
        for half in range(2):
            low = half * pixel_count + piece * main
            out[:, low : low + main] = total[half * held : (half + 1) * held, 0:main].astype(bf16)
        tails.append(total[:, main : main + share])
    left = pixel_count - pieces * main
    if left:
        tail = jnp.concatenate(tails, axis=1)[:, 0:left]
        for half in range(2):
            low = half * pixel_count + pieces * main
            out[:, low : low + left] = tail[half * held : (half + 1) * held].astype(bf16)


def expectation(particles, projections, ctf, defocus_group, offsets, routes):
    pixel_count = KX * KY
    rows = particles.shape[0]
    route_count = routes.shape[1]
    held = projections.shape[0] * projections.shape[1]
    far, near, cores, columns = (
        lax.axis_size(name) for name in ("far", "near", "core", "cls")
    )
    group = ("near", "cls")
    same_core = ("far", "near", "cls")
    pieces = near * columns
    peers = far * pieces
    owners = peers * cores
    plan = layout(pixel_count, pieces, route_count + 1)
    main, share, width, spare = plan
    place = lax.axis_index(group)
    total = held * owners
    params = pltpu.CompilerParams(vmem_limit_bytes=min(60 << 20, (8 << 20) + total * (88 << 10)))

    steps = [0] + sorted(range(1, pieces), key=exchange_order)
    distant = (
        projections.reshape(held, 2 * pixel_count),
        particles,
        ctf,
        defocus_group[None, :],
        offsets.T,
        routes.T,
    )
    split = jax.ShapeDtypeStruct((peers, 2 * held, width), bf16)
    piece = jax.ShapeDtypeStruct((2 * rows, width), bf16)
    in_place = pl.BlockSpec(memory_space=pltpu.HBM)
    own = jax.ShapeDtypeStruct((ctf.shape[0], width), bf16)
    refs, ctf_here, *parts = pl.pallas_call(
        functools.partial(prepare_kernel, pixel_count, plan, steps, group),
        out_shape=[split, own] + [piece] * pieces,
        in_specs=[in_place] * len(distant),
        out_specs=[in_place] * (2 + pieces),
        scratch_shapes=[pltpu.VMEM(array.shape, array.dtype) for array in distant]
        + [
            pltpu.VMEM(split.shape, bf16),
            pltpu.VMEM(own.shape, bf16),
            pltpu.VMEM((pieces, 2 * rows, width), bf16),
            pltpu.VMEM((rows, pixel_count), f32),
            pltpu.VMEM((-(-(3 + route_count) // 8) * 8, -(-rows // LANES) * LANES), f32),
            pltpu.SemaphoreType.DMA((len(distant),)),
            pltpu.SemaphoreType.DMA((2 + pieces,)),
        ],
        compiler_params=pltpu.CompilerParams(vmem_limit_bytes=60 << 20),
        name="prepare",
    )(*distant)
    refs = lax.all_to_all(refs, same_core, split_axis=0, concat_axis=0, tiled=True)
    blocks = [refs] + [lax.ppermute(refs, "core", routes_of(step, cores)) for step in range(1, cores)]
    blocks = [block.transpose(1, 0, 2) for block in blocks]
    parts = list(parts)
    for at in range(1, pieces):
        parts[at] = lax.ppermute(parts[at], group, routes_of(steps[at], pieces))

    lane = jnp.arange(width, dtype=jnp.int32)
    column = lane + jnp.where(lane < main, place * main, (pieces - 1) * main + place * share)
    across, down = column // KY, column % KY - KY // 2
    angles = jnp.stack([across, down]).astype(f32) * (2.0 * math.pi / BOX)
    phases = jnp.stack([jnp.cos(angles), jnp.sin(angles)], axis=1).reshape(4, width)
    count = pieces * rows
    listings = route_count * SHIFTS * held * columns
    folds = 4 if count % 32 == 0 else 1
    turned, energies = zip(
        *(
            pl.pallas_call(
                turn_kernel,
                out_shape=(
                    jax.ShapeDtypeStruct((2, SHIFTS * held * peers, width), bf16),
                    jax.ShapeDtypeStruct((ctf.shape[0], SHIFTS * held * peers), f32),
                ),
                scratch_shapes=[pltpu.VMEM((held * peers, width), f32)],
                compiler_params=params,
            )(block, ctf_here, phases)
            for block in blocks
        )
    )
    scores, aligned = pl.pallas_call(
        functools.partial(score_kernel, rows, route_count, columns, held, cores, steps, spare),
        out_shape=(
            jax.ShapeDtypeStruct((pieces, count // folds, folds * listings), f32),
            jax.ShapeDtypeStruct((pieces, 2 * rows, width), bf16),
        ),
        scratch_shapes=[
            pltpu.VMEM((count, SHIFTS * total), f32),
            pltpu.VMEM((count, LANES), f32),
            pltpu.VMEM((count // folds, folds * listings), f32),
        ],
        compiler_params=params,
        name="score",
    )(*parts, *turned, *energies)
    aligned = aligned.reshape(pieces * 2 * rows, width)

    scores = lax.all_to_all(scores, group, split_axis=0, concat_axis=0, tiled=True)

    each = SHIFTS * held * peers
    block = (2 * held, peers, width)
    *sums, own_real, own_imag, evidence = pl.pallas_call(
        functools.partial(weigh_kernel, rows, route_count, columns, held, cores, spare),
        out_shape=(
            *[jax.ShapeDtypeStruct(block, bf16)] * (cores - 1),
            *[jax.ShapeDtypeStruct((each, 2 * count), bf16)] * 2,
            jax.ShapeDtypeStruct((2 * count, LANES), f32),
        ),
        scratch_shapes=[pltpu.VMEM((count, listings), f32), pltpu.VMEM((2 * count, listings), f32)],
        compiler_params=params,
        name="weigh",
    )(scores, aligned, phases)
    sums = [
        lax.ppermute(array, "core", routes_of(step, cores))
        for step, array in enumerate(sums, 1)
    ]
    merged = pl.pallas_call(
        own_kernel,
        out_shape=jax.ShapeDtypeStruct(block, f32),
        compiler_params=params,
        cost_estimate=pl.CostEstimate(
            flops=8 * each * count * width, bytes_accessed=4 << 20, transcendentals=0
        ),
        name="own",
    )(own_real, own_imag, aligned, phases)
    log_evidence = lax.dynamic_slice_in_dim(evidence, place * 2 * rows, rows, 0)[:, 0]

    for array in sums:
        merged = merged + array.astype(f32)
    merged = merged.astype(bf16).transpose(1, 0, 2)
    merged = lax.all_to_all(merged, same_core, split_axis=0, concat_axis=0, tiled=True)
    data_sum = pl.pallas_call(
        functools.partial(collect_kernel, far, main, share),
        out_shape=jax.ShapeDtypeStruct((held, 2 * pixel_count), bf16),
        compiler_params=params,
        name="collect",
    )(merged)
    return (log_evidence, data_sum.reshape(projections.shape))


def solution(mesh):
    groups, orient, columns = (mesh.shape[name] for name in ("groups", "orient", "cls"))
    cores = 2 if orient % 2 == 0 else 1
    near = 2 if orient % (2 * cores) == 0 else 1
    axes = ("groups", "far", "near", "core", "cls")
    along = ("far", "near", "core")
    inner = Mesh(
        mesh.devices.reshape(groups, orient // (near * cores), near, cores, columns), axes
    )
    placed = (
        P(axes, None),
        P("cls", along, None),
        P(),
        P(axes),
        P(axes, None),
        P(axes, None),
    )
    return jax.shard_map(
        expectation,
        mesh=inner,
        in_specs=placed,
        out_specs=(P(axes), P(("groups", "cls"), along, None)),
        check_vma=False,
    )
```

```python
import functools
import math

import jax
import jax.numpy as jnp
from jax import lax
from jax.experimental import pallas as pl
from jax.experimental.pallas import tpu as pltpu
from jax.sharding import Mesh
from jax.sharding import PartitionSpec as P


KX = 86
KY = 192
BOX = 256
LANES = 128
SHIFTS = 5

highest = lax.Precision.HIGHEST
f32 = jnp.float32
bf16 = jnp.bfloat16


def unit_circle(turns):
    quarter = BOX // 4
    quadrant = jnp.floor(turns * (1.0 / quarter) + 0.5)
    angle = (turns - quadrant * quarter) * (2.0 * math.pi / BOX)
    quadrant = quadrant - 4.0 * jnp.floor(quadrant * 0.25)
    square = angle * angle
    sine = angle * (
        1.0
        + square
        * (-1.0 / 6 + square * (1.0 / 120 + square * (-1.0 / 5040 + square * (1.0 / 362880))))
    )
    cosine = 1.0 + square * (
        -0.5 + square * (1.0 / 24 + square * (-1.0 / 720 + square * (1.0 / 40320)))
    )
    odd = (quadrant == 1.0) | (quadrant == 3.0)
    first = jnp.where(odd, sine, cosine)
    second = jnp.where(odd, cosine, sine)
    first = jnp.where((quadrant == 1.0) | (quadrant == 2.0), -first, first)
    second = jnp.where(quadrant >= 2.0, -second, second)
    return first, second


def other(place, step, size):
    if size & (size - 1) == 0:
        return place ^ step
    return lax.rem(place + step, size)


def source(place, step, size):
    if size & (size - 1) == 0:
        return place ^ step
    return lax.rem(place + size - step, size)


def exchange_order(step):
    return (step.bit_count() == 2, -step.bit_count(), step)


def routes_of(step, size):
    return [(i, int(other(i, step, size))) for i in range(size)]


def layout(pixel_count, pieces, facts):
    main = pixel_count // (pieces * LANES) * LANES
    share = -(-(pixel_count - pieces * main) // pieces)
    width = main + LANES * (1 if share + facts <= LANES else 2)
    return main, share, width, share if width == main + LANES else 0


def split_refs(pixel_count, main, share, refs, out):
    held, width = refs.shape[0], out.shape[2]
    pieces = pixel_count // main if share == 0 else (pixel_count - 1) // (main + share) + 1
    for half in range(2):
        start = half * pixel_count
        left = refs[:, start + pieces * main : start + pixel_count].astype(f32)
        for piece in range(pieces):
            tail = left[:, piece * share : (piece + 1) * share]
            empty = jnp.zeros((held, width - main - tail.shape[1]), f32)
            tail = jnp.concatenate([tail, empty], axis=1).astype(bf16)
            values = refs[:, start + piece * main : start + (piece + 1) * main]
            for copy in range(piece, out.shape[0], pieces):
                out[copy, half * held : (half + 1) * held, 0:main] = values
                out[copy, half * held : (half + 1) * held, main:width] = tail


def own_ctf(pixel_count, plan, pieces, place, ctf, out):
    main, share, width, _ = plan
    for low in range(0, main, LANES):
        start = pl.multiple_of(place * main + low, LANES)
        out[:, low : low + LANES] = ctf[:, pl.ds(start, LANES)]
    left = ctf[:, pieces * main : pixel_count].astype(f32)
    tail = jnp.zeros((ctf.shape[0], width - main), f32)
    for piece in range(pieces):
        mine = left[:, piece * share : (piece + 1) * share]
        empty = jnp.zeros((ctf.shape[0], width - main - mine.shape[1]), f32)
        tail = jnp.where(place == piece, jnp.concatenate([mine, empty], axis=1), tail)
    out[:, main:width] = tail.astype(bf16)


def prepare_kernel(pixel_count, plan, steps, group, *refs):
    distant, (split, ctf_out, *outs), rest = refs[:6], refs[6 : 8 + len(steps)], refs[8 + len(steps) :]
    near, (split_here, ctf_here, whole, ctf_rows, table, arrived, left) = rest[:6], rest[6:]
    copies = [
        pltpu.make_async_copy(far, here, arrived.at[i])
        for i, (far, here) in enumerate(zip(distant, near))
    ]
    for copy in copies:
        copy.start()
    copies[0].wait()
    split_refs(pixel_count, *plan[:2], near[0], split_here)
    sent = [pltpu.make_async_copy(split_here, split, left.at[0])]
    sent[0].start()
    for copy in copies[2:]:
        copy.wait()
    place = lax.axis_index(group)
    own_ctf(pixel_count, plan, len(steps), place, near[2], ctf_here)
    sent.append(pltpu.make_async_copy(ctf_here, ctf_out, left.at[1]))
    sent[1].start()
    align(pixel_count, plan, *near[1:], whole, ctf_rows, table, copies[1])
    for step, out in zip(steps, outs):
        piece = whole.at[other(place, step, len(steps))]
        sent.append(pltpu.make_async_copy(piece, out, left.at[len(sent)]))
        sent[-1].start()
    for copy in sent:
        copy.wait()


def align(
    pixel_count, plan, images, ctf, groups, offsets, routes, whole, ctf_rows, table, coming
):
    rows = images.shape[0]
    pieces = whole.shape[0]
    route_count = routes.shape[0]
    table[...] = jnp.zeros(table.shape, f32)
    table[0:2, 0:rows] = offsets[...].astype(f32)
    table[2:3, 0:rows] = groups[...].astype(f32)
    table[3 : 3 + route_count, 0:rows] = routes[...].astype(f32)
    facts = table[...].T[0:rows]
    shift_across, shift_down, group = facts[:, 0:1], facts[:, 1:2], facts[:, 2:3]
    block = math.lcm(LANES, KY)
    per_block = block // LANES
    onehot = (
        group == lax.broadcasted_iota(jnp.int32, (rows, ctf.shape[0]), 1).astype(f32)
    ).astype(bf16)
    ctf_rows[...] = jnp.dot(onehot, ctf[...], preferred_element_type=f32)
    lane = lax.broadcasted_iota(jnp.int32, (rows, block), 1)
    across = jnp.zeros((rows, block), jnp.int32)
    for step in range(1, block // KY):
        across = across + (lane >= step * KY).astype(jnp.int32)
    down = lane - across * KY - KY // 2
    base_cos, base_sin = unit_circle(
        across.astype(f32) * shift_across + down.astype(f32) * shift_down
    )
    blocks = -(-pixel_count // block)
    start = lax.broadcasted_iota(jnp.int32, (rows, blocks), 1) * (block // KY)
    start_cos, start_sin = unit_circle(start.astype(f32) * shift_across)
    coming.wait()

    def tile(low):
        turn, step = divmod(low // LANES, per_block)
        bc = base_cos[:, step * LANES : (step + 1) * LANES]
        bs = base_sin[:, step * LANES : (step + 1) * LANES]
        rc = start_cos[:, turn : turn + 1]
        rs = start_sin[:, turn : turn + 1]
        cosine = bc * rc - bs * rs
        sine = bs * rc + bc * rs
        scale = ctf_rows[:, low : low + LANES]
        real = images[:, low : low + LANES].astype(f32)
        imag = images[:, pixel_count + low : pixel_count + low + LANES].astype(f32)
        first = (real * cosine + imag * sine) * scale
        second = (imag * cosine - real * sine) * scale
        return jnp.concatenate([first, second], axis=0)

    main, share, width, spare = plan
    for piece in range(pieces):
        for low in range(0, main, LANES):
            whole[piece, :, low : low + LANES] = tile(piece * main + low).astype(bf16)
    left = [tile(low) for low in range(pieces * main, pixel_count, LANES)]
    lane = lax.broadcasted_iota(jnp.int32, (rows, LANES), 1)
    notes = jnp.where(lane == spare + route_count, group, 0.0)
    for r in range(route_count):
        notes = jnp.where(lane == spare + r, facts[:, 3 + r : 4 + r], notes)
    notes = jnp.concatenate([notes, notes], axis=0)
    left = jnp.concatenate(left, axis=1) if left else notes[:, 0:0]
    for piece in range(pieces):
        mine = left[:, piece * share : (piece + 1) * share]
        if width > main + LANES:
            empty = jnp.zeros((2 * rows, width - LANES - main - mine.shape[1]), f32)
            tail = jnp.concatenate([mine, empty, notes], axis=1)
        else:
            tail = jnp.concatenate([mine, notes[:, mine.shape[1] :]], axis=1)
        whole[piece, :, main:width] = tail.astype(bf16)


def spot_table(spot, spots):
    row = lax.broadcasted_iota(jnp.int32, (spots, spot.shape[1]), 0).astype(f32)
    return jnp.where(row == spot, 1.0, 0.0).astype(bf16)


def block_facts(held, peers, blocks, columns, core_here):
    each = SHIFTS * held * peers
    lane = lax.broadcasted_iota(jnp.int32, (1, each * blocks), 1)
    inside, peer = lax.rem(lane, each), lax.rem(lane, peers)
    core = source(core_here, lane // each, blocks)
    direction = (peer // columns) * blocks + core
    spot = (inside // peers) * columns + lax.rem(peer, columns)
    return direction.astype(f32), spot.astype(f32)


def turn_kernel(refs, ctf, phases, turned, energy, power):
    width = phases.shape[1]
    held = refs.shape[0] // 2
    total = held * refs.shape[1]
    for low in range(0, width, LANES):
        here = slice(low, low + LANES)
        real = jnp.concatenate([refs[k, :, here] for k in range(held)], axis=0)
        imag = jnp.concatenate([refs[held + k, :, here] for k in range(held)], axis=0)
        turned[0, 0:total, here] = real
        turned[1, 0:total, here] = imag
        real, imag = real.astype(f32), imag.astype(f32)
        power[:, here] = real * real + imag * imag
        for axis in range(2):
            cosine = phases[2 * axis : 2 * axis + 1, here]
            sine = phases[2 * axis + 1 : 2 * axis + 2, here]
            rc, rs, ic, is_ = real * cosine, real * sine, imag * cosine, imag * sine
            at = (1 + 2 * axis) * total
            turned[0, at : at + total, here] = (rc - is_).astype(bf16)
            turned[1, at : at + total, here] = (rs + ic).astype(bf16)
            at = at + total
            turned[0, at : at + total, here] = (rc + is_).astype(bf16)
            turned[1, at : at + total, here] = (ic - rs).astype(bf16)
    table = ctf[...].astype(f32)
    half = 0.5 * lax.dot_general(
        table * table,
        power[...],
        (((1,), (1,)), ((), ())),
        precision=highest,
        preferred_element_type=f32,
    )
    energy[...] = jnp.concatenate([half] * SHIFTS, axis=1)


def score_kernel(rows, route_count, columns, held, cores, steps, spare, *refs_all):
    count = len(steps)
    parts, blocks, energies = refs_all[:count], refs_all[count:][:cores], refs_all[count + cores :][:cores]
    out, aligned, dense, notes, packed = refs_all[count + 2 * cores :]
    place, core = lax.axis_index(("near", "cls")), lax.axis_index("core")
    width = blocks[0].shape[2]
    each = blocks[0].shape[1]
    for step, part in zip(steps, parts):
        aligned[source(place, step, count)] = part[...]
    across = (((1,), (1,)), ((), ()))
    images = aligned[:, :, 0:width].reshape(2 * rows * count, width)
    for block, turned in enumerate(blocks):
        real = lax.dot_general(images, turned[0], across, preferred_element_type=f32)
        imag = lax.dot_general(images, turned[1], across, preferred_element_type=f32)
        for at in range(count):
            low = 2 * rows * at
            dense[at * rows : (at + 1) * rows, block * each : (block + 1) * each] = (
                real[low : low + rows, :] + imag[low + rows : low + 2 * rows, :]
            )
    for at in range(count):
        mine = slice(at * rows, (at + 1) * rows)
        notes[mine, :] = aligned[at, 0:rows, width - LANES : width].astype(f32)
    energy = jnp.concatenate([energy[...] for energy in energies], axis=1)
    facts = notes[...]
    values = dense[...]
    for g in range(energy.shape[0]):
        values = values - jnp.where(
            facts[:, spare + route_count : spare + route_count + 1] == float(g), energy[g : g + 1, :], 0.0
        )
    first = values.astype(bf16)
    rest = values - first.astype(f32)
    second = rest.astype(bf16)
    third = (rest - second.astype(f32)).astype(bf16)
    terms = [first.astype(f32), second.astype(f32), third.astype(f32)]
    direction, spot = block_facts(held, each // (SHIFTS * held), cores, columns, core)
    spots = SHIFTS * held * columns
    particles = rows * count
    stacked = []
    for r in range(route_count):
        listed = facts[:, spare + r : spare + r + 1] == direction
        stacked += [jnp.where(listed, term, 0.0).astype(bf16) for term in terms]
    chosen = lax.dot_general(
        jnp.concatenate(stacked, axis=0),
        spot_table(spot, spots),
        across,
        preferred_element_type=f32,
    )
    height = out.shape[1]
    for r in range(route_count):
        low = r * len(terms) * particles
        mine = chosen[low : low + particles]
        for term in range(1, len(terms)):
            mine = mine + chosen[low + term * particles : low + (term + 1) * particles]
        for block in range(particles // height):
            at = (block * route_count + r) * spots
            packed[:, at : at + spots] = mine[block * height : (block + 1) * height]
    for copy in range(out.shape[0]):
        out[copy] = packed[...]


def turn_back(weights_real, weights_imag, aligned, phases, out):
    width = phases.shape[1]
    held, peers = out.shape[0] // 2, out.shape[1]
    total = held * peers
    weights = jnp.concatenate([weights_real, weights_imag], axis=0)
    chunk = 6 * LANES
    for low in range(0, width, chunk):
        high = min(low + chunk, width)
        images = aligned[:, low:high]
        both = jnp.dot(weights, images, preferred_element_type=f32)
        real, imag = both[: SHIFTS * total], both[SHIFTS * total :]
        u = [real[t * total : (t + 1) * total] for t in range(SHIFTS)]
        v = [imag[t * total : (t + 1) * total] for t in range(SHIFTS)]
        first, second = u[0], v[0]
        for axis in range(2):
            cosine = phases[2 * axis : 2 * axis + 1, low:high]
            sine = phases[2 * axis + 1 : 2 * axis + 2, low:high]
            one, two = 1 + 2 * axis, 2 + 2 * axis
            first = first + (u[one] + u[two]) * cosine + (v[one] - v[two]) * sine
            second = second + (v[one] + v[two]) * cosine - (u[one] - u[two]) * sine
        for k in range(held):
            mine = slice(k * peers, (k + 1) * peers)
            out[k, :, low:high] = first[mine].astype(out.dtype)
            out[held + k, :, low:high] = second[mine].astype(out.dtype)


def weigh_kernel(rows, route_count, columns, held, cores, spare, scores, aligned, phases, *outs_and_scratch):
    core = lax.axis_index("core")
    *outs, own_real, own_imag, evidence, tall, wide = outs_and_scratch
    width = phases.shape[1]
    count = aligned.shape[0]
    each = own_real.shape[0]
    peers = each // (SHIFTS * held)
    height = scores.shape[1]
    blocks = count // (2 * height)
    listings = scores.shape[2] // blocks
    summed = scores[0]
    for part in range(1, scores.shape[0]):
        summed = summed + scores[part]
    for block in range(blocks):
        tall[block * height : (block + 1) * height, :] = summed[
            :, block * listings : (block + 1) * listings
        ]
    for part in range(count // (2 * rows)):
        values = tall[part * rows : (part + 1) * rows, :]
        at = 2 * rows * part
        wide[at : at + rows, :] = values
        wide[at + rows : at + 2 * rows, :] = values
    values = wide[...]
    peak = jnp.max(values, axis=1, keepdims=True)
    mass = jnp.sum(jnp.exp(values - peak), axis=1, keepdims=True)
    log_evidence = peak + jnp.log(mass)
    evidence[...] = jnp.broadcast_to(log_evidence, evidence.shape)
    listed_weights = jnp.exp(values - log_evidence).astype(bf16)
    notes = aligned[:, width - LANES : width].astype(f32)
    direction, spot = block_facts(held, peers, cores, columns, core)
    spots = listings // route_count
    spread = spot_table(spot, spots)
    weights = jnp.zeros((count, each * cores), f32)
    for r in range(route_count):
        placed = jnp.dot(
            listed_weights[:, r * spots : (r + 1) * spots], spread, preferred_element_type=f32
        )
        weights = jnp.where(notes[:, spare + r : spare + r + 1] == direction, placed, weights)
    row = lax.broadcasted_iota(jnp.int32, (count, 1), 0)
    first_half = jnp.zeros((count, 1), jnp.bool_)
    for part in range(count // (2 * rows)):
        at = 2 * rows * part
        first_half = first_half | ((row >= at) & (row < at + rows))
    weights_real = jnp.where(first_half, weights, 0.0).T.astype(bf16)
    weights_imag = jnp.where(first_half, 0.0, weights).T.astype(bf16)
    own_real[...] = weights_real[0:each]
    own_imag[...] = weights_imag[0:each]
    for step, out in enumerate(outs, 1):
        block = slice(step * each, (step + 1) * each)
        turn_back(weights_real[block], weights_imag[block], aligned, phases, out)


def own_kernel(weights_real, weights_imag, aligned, phases, out):
    turn_back(weights_real[...], weights_imag[...], aligned, phases, out)


def collect_kernel(far, main, share, parts, out):
    pieces, held = parts.shape[0] // far, out.shape[0]
    pixel_count = out.shape[1] // 2
    tails = []
    for piece in range(pieces):
        total = parts[piece].astype(f32)
        for part in range(1, far):
            total = total + parts[part * pieces + piece].astype(f32)
        for half in range(2):
            low = half * pixel_count + piece * main
            out[:, low : low + main] = total[half * held : (half + 1) * held, 0:main].astype(bf16)
        tails.append(total[:, main : main + share])
    left = pixel_count - pieces * main
    if left:
        tail = jnp.concatenate(tails, axis=1)[:, 0:left]
        for half in range(2):
            low = half * pixel_count + pieces * main
            out[:, low : low + left] = tail[half * held : (half + 1) * held].astype(bf16)


def expectation(particles, projections, ctf, defocus_group, offsets, routes):
    pixel_count = KX * KY
    rows = particles.shape[0]
    route_count = routes.shape[1]
    held = projections.shape[0] * projections.shape[1]
    far, near, cores, columns = (
        lax.axis_size(name) for name in ("far", "near", "core", "cls")
    )
    group = ("near", "cls")
    same_core = ("far", "near", "cls")
    pieces = near * columns
    peers = far * pieces
    owners = peers * cores
    plan = layout(pixel_count, pieces, route_count + 1)
    main, share, width, spare = plan
    place = lax.axis_index(group)
    total = held * owners
    params = pltpu.CompilerParams(vmem_limit_bytes=min(60 << 20, (8 << 20) + total * (88 << 10)))

    steps = [0] + sorted(range(1, pieces), key=exchange_order)
    distant = (
        projections.reshape(held, 2 * pixel_count),
        particles,
        ctf,
        defocus_group[None, :],
        offsets.T,
        routes.T,
    )
    split = jax.ShapeDtypeStruct((peers, 2 * held, width), bf16)
    piece = jax.ShapeDtypeStruct((2 * rows, width), bf16)
    in_place = pl.BlockSpec(memory_space=pltpu.HBM)
    own = jax.ShapeDtypeStruct((ctf.shape[0], width), bf16)
    refs, ctf_here, *parts = pl.pallas_call(
        functools.partial(prepare_kernel, pixel_count, plan, steps, group),
        out_shape=[split, own] + [piece] * pieces,
        in_specs=[in_place] * len(distant),
        out_specs=[in_place] * (2 + pieces),
        scratch_shapes=[pltpu.VMEM(array.shape, array.dtype) for array in distant]
        + [
            pltpu.VMEM(split.shape, bf16),
            pltpu.VMEM(own.shape, bf16),
            pltpu.VMEM((pieces, 2 * rows, width), bf16),
            pltpu.VMEM((rows, pixel_count), f32),
            pltpu.VMEM((-(-(3 + route_count) // 8) * 8, -(-rows // LANES) * LANES), f32),
            pltpu.SemaphoreType.DMA((len(distant),)),
            pltpu.SemaphoreType.DMA((2 + pieces,)),
        ],
        compiler_params=pltpu.CompilerParams(vmem_limit_bytes=60 << 20),
        name="prepare",
    )(*distant)
    refs = lax.all_to_all(refs, same_core, split_axis=0, concat_axis=0, tiled=True)
    blocks = [refs] + [lax.ppermute(refs, "core", routes_of(step, cores)) for step in range(1, cores)]
    blocks = [block.transpose(1, 0, 2) for block in blocks]
    parts = list(parts)
    for at in range(1, pieces):
        parts[at] = lax.ppermute(parts[at], group, routes_of(steps[at], pieces))

    lane = jnp.arange(width, dtype=jnp.int32)
    column = lane + jnp.where(lane < main, place * main, (pieces - 1) * main + place * share)
    across, down = column // KY, column % KY - KY // 2
    angles = jnp.stack([across, down]).astype(f32) * (2.0 * math.pi / BOX)
    phases = jnp.stack([jnp.cos(angles), jnp.sin(angles)], axis=1).reshape(4, width)
    count = pieces * rows
    listings = route_count * SHIFTS * held * columns
    folds = 4 if count % 32 == 0 else 1
    turned, energies = zip(
        *(
            pl.pallas_call(
                turn_kernel,
                out_shape=(
                    jax.ShapeDtypeStruct((2, SHIFTS * held * peers, width), bf16),
                    jax.ShapeDtypeStruct((ctf.shape[0], SHIFTS * held * peers), f32),
                ),
                scratch_shapes=[pltpu.VMEM((held * peers, width), f32)],
                compiler_params=params,
            )(block, ctf_here, phases)
            for block in blocks
        )
    )
    scores, aligned = pl.pallas_call(
        functools.partial(score_kernel, rows, route_count, columns, held, cores, steps, spare),
        out_shape=(
            jax.ShapeDtypeStruct((pieces, count // folds, folds * listings), f32),
            jax.ShapeDtypeStruct((pieces, 2 * rows, width), bf16),
        ),
        scratch_shapes=[
            pltpu.VMEM((count, SHIFTS * total), f32),
            pltpu.VMEM((count, LANES), f32),
            pltpu.VMEM((count // folds, folds * listings), f32),
        ],
        compiler_params=params,
        name="score",
    )(*parts, *turned, *energies)
    aligned = aligned.reshape(pieces * 2 * rows, width)

    scores = lax.all_to_all(scores, group, split_axis=0, concat_axis=0, tiled=True)

    each = SHIFTS * held * peers
    block = (2 * held, peers, width)
    *sums, own_real, own_imag, evidence = pl.pallas_call(
        functools.partial(weigh_kernel, rows, route_count, columns, held, cores, spare),
        out_shape=(
            *[jax.ShapeDtypeStruct(block, bf16)] * (cores - 1),
            *[jax.ShapeDtypeStruct((each, 2 * count), bf16)] * 2,
            jax.ShapeDtypeStruct((2 * count, LANES), f32),
        ),
        scratch_shapes=[pltpu.VMEM((count, listings), f32), pltpu.VMEM((2 * count, listings), f32)],
        compiler_params=params,
        name="weigh",
    )(scores, aligned, phases)
    sums = [
        lax.ppermute(array, "core", routes_of(step, cores))
        for step, array in enumerate(sums, 1)
    ]
    merged = pl.pallas_call(
        own_kernel,
        out_shape=jax.ShapeDtypeStruct(block, f32),
        compiler_params=params,
        cost_estimate=pl.CostEstimate(
            flops=8 * each * count * width, bytes_accessed=4 << 20, transcendentals=0
        ),
        name="own",
    )(own_real, own_imag, aligned, phases)
    log_evidence = lax.dynamic_slice_in_dim(evidence, place * 2 * rows, rows, 0)[:, 0]

    for array in sums:
        merged = merged + array.astype(f32)
    merged = merged.astype(bf16).transpose(1, 0, 2)
    merged = lax.all_to_all(merged, same_core, split_axis=0, concat_axis=0, tiled=True)
    data_sum = pl.pallas_call(
        functools.partial(collect_kernel, far, main, share),
        out_shape=jax.ShapeDtypeStruct((held, 2 * pixel_count), bf16),
        compiler_params=params,
        name="collect",
    )(merged)
    return (log_evidence, data_sum.reshape(projections.shape))


def solution(mesh):
    groups, orient, columns = (mesh.shape[name] for name in ("groups", "orient", "cls"))
    cores = 2 if orient % 2 == 0 else 1
    near = 2 if orient % (2 * cores) == 0 else 1
    axes = ("groups", "far", "near", "core", "cls")
    along = ("far", "near", "core")
    inner = Mesh(
        mesh.devices.reshape(groups, orient // (near * cores), near, cores, columns), axes
    )
    placed = (
        P(axes, None),
        P("cls", along, None),
        P(),
        P(axes),
        P(axes, None),
        P(axes, None),
    )
    return jax.shard_map(
        expectation,
        mesh=inner,
        in_specs=placed,
        out_specs=(P(axes), P(("groups", "cls"), along, None)),
        check_vma=False,
    )
```
